32 devices in a mesh: row: 8 (over z, core), rep: 4 (over y, x).
Axes of the slice: x: 2, y: 2, z: 4, core: 2. Of those that a mesh axis runs over, the one named last changes fastest.
Arguments:
- features: bfloat16 [1024, 512], P('row', 'rep'), may hold values from -6 to 6
- edge_tiles: bfloat16 [8, 8, 128, 128], P('row'), may hold values from -0.3125 to 0.3125
- sources: int32 [8, 8], P('row'), may hold values from 0 to 7, as said below
- counts: int32 [8], P('row'), may hold values from 1 to 8, as said below
- w_first: bfloat16 [512, 512], P('rep'), may hold values from -0.25 to 0.25
- w_second: bfloat16 [512, 512], P('rep'), may hold values from -0.25 to 0.25
- cotangent: bfloat16 [1024, 512], P('row', 'rep'), may hold values from -6 to 6
Outputs:
- embeddings: bfloat16 [1024, 512], P('row', 'rep')
- grad_first: float32 [512, 512], P('rep')
- grad_second: float32 [512, 512], P('rep')
The draws below stay inside these ranges and needn't reach their ends.
Inputs may be any that keep to these rules, and one draw needn't show every extreme that they name: `sources`: the 8 source blocks of one block row are distinct. `counts`: some block row has all 8 slots live.
All inputs are finite; a program needn't handle non-finite values.
Results may differ from the reference program's by a relative error of at most 0.0065.
Values may be sent and summed in bfloat16 or wider, within the bound.
No kernel may reach another device: no remote copies, remote signals or barrier semaphores. Data moves between devices by JAX's collectives and lax.ppermute only.
A program may use at most 64 MiB of HBM per device.

```python
import math
import jax
import jax.numpy as jnp
from jax import lax

D = 512
BLOCK = 128
N_BLOCKS = 8
N_NODES = 1024
KMAX = 8


def draw_sources(key, part):
    keys = jax.random.split(key, N_BLOCKS)
    return jax.vmap(lambda single: jax.random.permutation(single, N_BLOCKS)[:KMAX])(keys).astype(jnp.int32)


def draw_counts(key, part):
    first, second, third = jax.random.split(key, 3)
    lower = jnp.minimum(jax.random.randint(first, (N_BLOCKS,), 1, KMAX + 1), jax.random.randint(second, (N_BLOCKS,), 1, KMAX + 1))
    place = jax.random.randint(third, (), 0, N_BLOCKS)
    return jnp.where(jnp.arange(N_BLOCKS) == place, KMAX, lower).astype(jnp.int32)


def block_scale(rng, extent, cuts, low, high):
    factor_of = 1.0
    for axis_at, blocks in cuts:
        steps = jax.random.uniform(jax.random.fold_in(jax.random.fold_in(rng, 6), axis_at), (blocks,), jnp.float32, low / len(cuts), high / len(cuts))
        factor_of = factor_of * jnp.repeat(jnp.exp(steps), extent[axis_at] // blocks).reshape((-1,) + (1,) * (len(extent) - 1 - axis_at))
    return factor_of


def noise(rng, extent, deviation, reach, cuts=(), held_as=jnp.bfloat16):
    factor_of = block_scale(rng, extent, cuts, -0.22, 0.18) if cuts else 1.0
    values = jax.random.normal(rng, extent, jnp.float32) * deviation * factor_of
    return jnp.minimum(jnp.maximum(values, -reach), reach).astype(held_as)


def setup_inputs(seed: int = 0) -> dict:
    arg_keys = jax.random.split(jax.random.key(seed), 8)
    features = noise(arg_keys[0], (N_NODES, D), 1.0, 6.0, ((0, 8), (1, 4)))
    edge_tiles = noise(arg_keys[1], (N_BLOCKS, KMAX, BLOCK, BLOCK), (KMAX * BLOCK // 3) ** -0.5, 0.3125, ((0, 8),))
    sources = draw_sources(jax.random.fold_in(arg_keys[7], 71), 0)
    counts = draw_counts(jax.random.fold_in(arg_keys[7], 71), 0)
    w_first = noise(arg_keys[4], (D, D), D ** -0.5, 0.25, ((0, 4),))
    w_second = noise(arg_keys[5], (D, D), D ** -0.5, 0.25, ((0, 4),))
    cotangent = noise(arg_keys[6], (N_NODES, D), 1.0, 6.0, ((0, 8), (1, 4)))
    return {"features": features, "edge_tiles": edge_tiles, "sources": sources, "counts": counts, "w_first": w_first, "w_second": w_second, "cotangent": cotangent}


def silu_slope(value):
    sig = jax.nn.sigmoid(value)
    return sig * (1.0 + value * (1.0 - sig))

def live_tiles_of(edge_tiles, counts):
    live = jnp.arange(KMAX, dtype=jnp.int32)[None, :] < counts[:, None]
    return edge_tiles * live[:, :, None, None].astype(edge_tiles.dtype)

def aggregate(field, live_tiles, sources):
    blocks = field.reshape(N_BLOCKS, BLOCK, D)

    def one_row(pair):
        tiles, picks = pair
        return jnp.einsum('kij,kjf->if', tiles.astype(jnp.float32), blocks[picks].astype(jnp.float32))
    return lax.map(one_row, (live_tiles, sources)).reshape(N_NODES, D)

def aggregate_back(field, live_tiles, sources):
    blocks = field.reshape(N_BLOCKS, BLOCK, D)

    def one_row(carry, triple):
        tiles, picks, block_rows = triple
        contrib = jnp.einsum('kij,if->kjf', tiles.astype(jnp.float32), block_rows.astype(jnp.float32))
        return (carry.at[picks].add(contrib), None)
    start = jnp.zeros((N_BLOCKS, BLOCK, D), jnp.float32)
    total, _ = lax.scan(one_row, start, (live_tiles, sources, blocks))
    return total.reshape(N_NODES, D)

def reference(features, edge_tiles, sources, counts, w_first, w_second, cotangent):
    live_tiles = live_tiles_of(edge_tiles, counts)
    scale = jnp.float32(1.0 / math.sqrt(N_NODES))
    agg_first = aggregate(features, live_tiles, sources).astype(jnp.bfloat16)
    pre_first = jnp.dot(agg_first, w_first, preferred_element_type=jnp.float32)
    hidden = jax.nn.silu(pre_first).astype(jnp.bfloat16)
    agg_second = aggregate(hidden, live_tiles, sources).astype(jnp.bfloat16)
    embeddings = jnp.dot(agg_second, w_second, preferred_element_type=jnp.float32).astype(jnp.bfloat16)
    grad_second = jnp.dot(agg_second.T, cotangent, preferred_element_type=jnp.float32) * scale
    back_agg = jnp.dot(cotangent, w_second.T, preferred_element_type=jnp.float32).astype(jnp.bfloat16)
    back_hidden = aggregate_back(back_agg, live_tiles, sources)
    back_pre = (back_hidden * silu_slope(pre_first)).astype(jnp.bfloat16)
    grad_first = jnp.dot(agg_first.T, back_pre, preferred_element_type=jnp.float32) * scale
    return (embeddings, grad_first, grad_second)
```

```python
import functools
import math

import jax
import jax.numpy as jnp
from jax import lax
from jax.experimental import pallas as pl
from jax.experimental.pallas import tpu as pltpu
from jax.sharding import PartitionSpec as P

BF16 = jnp.bfloat16
F32 = jnp.float32
CORES = 2
REPLICATED_BYTES = 16 * 2**20


def silu_slope(value):
    sig = jax.nn.sigmoid(value)
    return sig * (1.0 + value * (1.0 - sig))


def gather_blocks(local, block):
    height, width = local.shape
    packed = local.reshape(height * width // 128, 128)
    whole = lax.all_gather(packed, "row", axis=0, tiled=True)
    return whole.reshape(-1, block, width)


def aggregate(local, live_tiles, sources):
    height, width = local.shape
    group_rows, slots, block, _ = live_tiles.shape
    blocks = gather_blocks(local, block)
    total = jnp.einsum(
        "bkij,bkjf->bif", live_tiles, blocks[sources], preferred_element_type=jnp.float32
    )
    return total.reshape(height, width).astype(jnp.bfloat16)


def spread_back(back_agg, live_tiles):
    group_rows, slots, block, _ = live_tiles.shape
    width = back_agg.shape[1]
    block_rows = back_agg.reshape(group_rows, block, width)
    return jnp.einsum("bkij,bif->bkjf", live_tiles, block_rows, preferred_element_type=jnp.float32)


def mix_columns(agg, weight):
    partial_terms = jnp.dot(agg, weight, preferred_element_type=jnp.float32)
    return lax.psum_scatter(partial_terms, "rep", scatter_dimension=1, tiled=True)


def widen(local):
    return lax.all_gather(local, "rep", axis=1, tiled=True)


def split_body(features, edge_tiles, sources, counts, w_first, w_second, cotangent):
    group_rows, slots, block, _ = edge_tiles.shape
    height, width = features.shape
    live = jnp.arange(slots, dtype=jnp.int32)[None, :] < counts[:, None]
    live_tiles = edge_tiles * live[:, :, None, None].astype(edge_tiles.dtype)
    scale = 1.0 / math.sqrt(height * lax.axis_size("row"))
    agg_first = aggregate(features, live_tiles, sources)
    pre_first = mix_columns(agg_first, w_first)
    hidden = jax.nn.silu(pre_first).astype(jnp.bfloat16)
    agg_second = aggregate(hidden, live_tiles, sources)
    embeddings = mix_columns(agg_second, w_second).astype(jnp.bfloat16)
    full_cotangent = widen(cotangent)
    second_part = jnp.dot(agg_second.T, full_cotangent, preferred_element_type=jnp.float32) * scale
    back_agg = jnp.dot(full_cotangent, w_second.T, preferred_element_type=jnp.float32).astype(
        jnp.bfloat16
    )
    contrib = spread_back(back_agg, live_tiles)
    flat_sources = sources.reshape(-1)
    flat_contrib = contrib.reshape(group_rows * slots, block * width)
    count = height * lax.axis_size("row")
    wanted = count // block
    inside = (flat_sources >= 0) & (flat_sources < wanted)
    target = jnp.where(inside, flat_sources, wanted)
    summed = jax.ops.segment_sum(flat_contrib, target, num_segments=wanted + 1)
    back_hidden = lax.psum_scatter(
        summed[:wanted].reshape(count, width), "row", scatter_dimension=0, tiled=True
    )
    back_pre = (back_hidden * silu_slope(pre_first)).astype(jnp.bfloat16)
    first_part = jnp.dot(agg_first.T, widen(back_pre), preferred_element_type=jnp.float32) * scale
    grad_second, grad_first = lax.psum((second_part, first_part), "row")
    return (embeddings, grad_first, grad_second)


def dot(a, b, contract):
    return lax.dot_general(a, b, (contract, ((), ())), preferred_element_type=F32)


def pack_kernel(chips, parts, sources_ref, counts_ref, feat_ref, cot_ref, tiles_ref, out_ref):
    _, slots, block, _ = tiles_ref.shape
    width = feat_ref.shape[1]
    out_ref[:, :width] = feat_ref[...]
    out_ref[:, width : 2 * width] = cot_ref[...]
    part = lax.axis_index("rep")
    for b in range(parts):
        position = part * parts + b
        node_block = lax.rem(position, chips) * CORES + lax.div(position, chips)
        slot = jnp.int32(slots)
        for k in range(slots):
            hit = jnp.logical_and(sources_ref[0, k] == node_block, k < counts_ref[0])
            slot = jnp.where(hit, jnp.int32(k), slot)
        tile = tiles_ref[0, jnp.minimum(slot, slots - 1)]
        keep = (slot < slots).astype(BF16)
        at = 2 * width + b * block
        out_ref[:, at : at + block] = tile * keep


def stack_kernel(chips, *refs):
    blocks, (w_first_ref, w_second_ref, out_ref, sems) = refs[:chips], refs[chips:]
    row = lax.axis_index("row")
    core, chip = lax.rem(row, CORES), lax.div(row, CORES)
    copies = [
        pltpu.make_async_copy(ref, out_ref.at[chip ^ d], sems.at[d]) for d, ref in enumerate(blocks)
    ]
    for copy in copies:
        copy.start()

    @pl.when(core == 0)
    def _():
        copy = pltpu.make_async_copy(w_first_ref, out_ref.at[chips], sems.at[chips])
        copy.start()
        copy.wait()

    @pl.when(core == 1)
    def _():
        copy = pltpu.make_async_copy(w_second_ref, out_ref.at[chips], sems.at[chips + 1])
        copy.start()
        copy.wait()

    for copy in copies:
        copy.wait()


def layers_kernel(chips, reps, scale, *refs):
    pieces = refs[: CORES * reps]
    emb_ref, gf_ref, gs_ref = refs[CORES * reps : CORES * reps + 3]
    a_s, f_s, c_s, w_s, af_s, hid_s, slope_s, ba_s, sems = refs[CORES * reps + 3 :]
    row, rep = lax.axis_index("row"), lax.axis_index("rep")
    core, chip = lax.rem(row, CORES), lax.div(row, CORES)
    height, width = emb_ref.shape
    nodes = CORES * chips * height
    share = nodes // reps
    half = chips * height

    copies = []
    for dc in range(CORES):
        for d in range(reps):
            piece = pieces[dc * reps + d]
            c, q = core ^ dc, rep ^ d
            lanes = pl.ds(pl.multiple_of(q * width, width), width)
            mine = piece.at[pl.ds(0, chips)]
            moves = (
                (mine.at[:, :, pl.ds(0, width)], f_s.at[c, :, :, lanes]),
                (mine.at[:, :, pl.ds(width, width)], c_s.at[c, :, :, lanes]),
                (
                    mine.at[:, :, pl.ds(2 * width, share)],
                    a_s.at[c, :, :, pl.ds(pl.multiple_of(q * share, share), share)],
                ),
                (piece.at[chips], w_s.at[c, lanes]),
            )
            for n, (src, dst) in enumerate(moves):
                copies.append(pltpu.make_async_copy(src, dst, sems.at[n, dc * reps + d]))
    for copy in copies:
        copy.start()
    for copy in copies:
        copy.wait()

    wide = f_s.shape[-1]
    a = a_s.reshape(nodes, nodes)
    feats = f_s.reshape(nodes, wide)
    cot = c_s.reshape(nodes, wide)
    my_cols = pl.ds(pl.multiple_of(rep * width, width), width)
    step = 2 * height

    def forward(i, _):
        rows = pl.ds(pl.multiple_of(i * step, step), step)
        agg = dot(a[rows, :], feats[...], ((1,), (0,))).astype(BF16)
        af_s[rows, :] = agg
        pre = dot(agg, w_s[0], ((1,), (0,)))
        sig = jax.nn.sigmoid(pre)
        hid_s[rows, :] = (pre * sig).astype(BF16)
        slope_s[rows, :] = sig * (1.0 + pre * (1.0 - sig))
        ba_s[rows, :] = dot(cot[rows, :], w_s[1], ((1,), (1,))).astype(BF16)
        return 0

    lax.fori_loop(0, nodes // step, forward, 0)

    gf_ref[...] = jnp.zeros_like(gf_ref)
    gs_ref[...] = jnp.zeros_like(gs_ref)

    def backward(i, _):
        start = pl.multiple_of(i * step, step)
        rows = pl.ds(start, step)
        back_hidden = dot(a[:, rows], ba_s[...], ((0,), (0,)))
        back_pre = (back_hidden * slope_s[rows, :]).astype(BF16)
        gf_ref[...] += dot(af_s[rows, my_cols], back_pre, ((0,), (0,)))
        agg = dot(a[rows, :], hid_s[:, my_cols], ((1,), (0,))).astype(BF16)
        gs_ref[...] += dot(agg, cot[rows, :], ((0,), (0,)))
        return 0

    lax.fori_loop(0, nodes // step, backward, 0)
    gf_ref[...] = gf_ref[...] * scale
    gs_ref[...] = gs_ref[...] * scale

    mine = pl.ds(pl.multiple_of((core * chips + chip) * height, height), height)
    agg_mine = dot(a[mine, :], hid_s[...], ((1,), (0,))).astype(BF16)
    emb_ref[...] = dot(agg_mine, w_s[1, :, my_cols], ((1,), (0,))).astype(BF16)


def whole_body(features, edge_tiles, sources, counts, w_first, w_second, cotangent):
    _, slots, block, _ = edge_tiles.shape
    height, width = features.shape
    rows, reps = lax.axis_size("row"), lax.axis_size("rep")
    chips = rows // CORES
    nodes = height * rows
    share = nodes // reps
    packed_width = 2 * width + share
    wide = width * reps
    anywhere = pl.BlockSpec(memory_space=pl.ANY)
    vmem = pl.BlockSpec(memory_space=pltpu.VMEM)
    smem = pl.BlockSpec(memory_space=pltpu.SMEM)

    packed = pl.pallas_call(
        functools.partial(pack_kernel, chips, share // block),
        out_shape=jax.ShapeDtypeStruct((height, packed_width), BF16),
        in_specs=[smem, smem, vmem, vmem, vmem],
        out_specs=vmem,
        name="pack",
    )(sources, counts, features, cotangent, edge_tiles)

    def swap(value, axis, size, d):
        return lax.ppermute(value, axis, [(i, i ^ d) for i in range(size)])

    blocks = [packed] + [swap(packed, "row", rows, CORES * d) for d in range(1, chips)]
    stacked = pl.pallas_call(
        functools.partial(stack_kernel, chips),
        out_shape=jax.ShapeDtypeStruct((chips + 1, height, packed_width), BF16),
        in_specs=[anywhere] * (chips + 2),
        out_specs=anywhere,
        scratch_shapes=[pltpu.SemaphoreType.DMA((chips + 2,))],
        name="stack",
    )(*blocks, w_first, w_second)
    pieces = [stacked] + [swap(stacked, "rep", reps, d) for d in range(1, reps)]
    pieces += [swap(piece, "row", rows, 1) for piece in pieces]

    return tuple(
        pl.pallas_call(
            functools.partial(layers_kernel, chips, reps, 1.0 / math.sqrt(nodes)),
            out_shape=(
                jax.ShapeDtypeStruct((height, width), BF16),
                jax.ShapeDtypeStruct((width, wide), F32),
                jax.ShapeDtypeStruct((width, wide), F32),
            ),
            in_specs=[anywhere] * (CORES * reps),
            out_specs=(vmem, vmem, vmem),
            scratch_shapes=[
                pltpu.VMEM((CORES, chips, height, nodes), BF16),
                pltpu.VMEM((CORES, chips, height, wide), BF16),
                pltpu.VMEM((CORES, chips, height, wide), BF16),
                pltpu.VMEM((CORES, wide, wide), BF16),
                pltpu.VMEM((nodes, wide), BF16),
                pltpu.VMEM((nodes, wide), BF16),
                pltpu.VMEM((nodes, wide), F32),
                pltpu.VMEM((nodes, wide), BF16),
                pltpu.SemaphoreType.DMA((4, CORES * reps)),
            ],
            name="layers",
        )(*pieces)
    )


def fits_whole(features, edge_tiles, rows, reps):
    nodes, wide = features.shape
    block = edge_tiles.shape[2]
    powers = all(n & (n - 1) == 0 for n in (rows, reps))
    held = 2 * (nodes * nodes + 2 * nodes * wide + 2 * wide * wide)
    width, share = wide // reps, nodes // reps
    return (
        held <= REPLICATED_BYTES
        and powers
        and rows % CORES == 0
        and nodes // rows == block == width
        and share % block == 0
        and 2 * width + share == wide
    )


def solution(mesh):
    placed = (
        P("row", "rep"),
        P("row", None, None, None),
        P("row", None),
        P("row"),
        P("rep", None),
        P("rep", None),
        P("row", "rep"),
    )

    def run(features, edge_tiles, *rest):
        whole = fits_whole(features, edge_tiles, mesh.shape["row"], mesh.shape["rep"])
        return jax.shard_map(
            whole_body if whole else split_body,
            mesh=mesh,
            in_specs=placed,
            out_specs=(P("row", "rep"), P("rep", None), P("rep", None)),
            check_vma=False,
        )(features, edge_tiles, *rest)

    return run
```

```python
import functools
import math

import jax
import jax.numpy as jnp
from jax import lax
from jax.experimental import pallas as pl
from jax.experimental.pallas import tpu as pltpu
from jax.sharding import PartitionSpec as P

BF16 = jnp.bfloat16
F32 = jnp.float32
CORES = 2
REPLICATED_BYTES = 16 * 2**20


def silu_slope(value):
    sig = jax.nn.sigmoid(value)
    return sig * (1.0 + value * (1.0 - sig))


def gather_blocks(local, block):
    height, width = local.shape
    packed = local.reshape(height * width // 128, 128)
    whole = lax.all_gather(packed, "row", axis=0, tiled=True)
    return whole.reshape(-1, block, width)


def aggregate(local, live_tiles, sources):
    height, width = local.shape
    _, _, block, _ = live_tiles.shape
    blocks = gather_blocks(local, block)
    total = jnp.einsum(
        "bkij,bkjf->bif", live_tiles, blocks[sources], preferred_element_type=jnp.float32
    )
    return total.reshape(height, width).astype(jnp.bfloat16)


def spread_back(back_agg, live_tiles):
    group_rows, _, block, _ = live_tiles.shape
    width = back_agg.shape[1]
    block_rows = back_agg.reshape(group_rows, block, width)
    return jnp.einsum("bkij,bif->bkjf", live_tiles, block_rows, preferred_element_type=jnp.float32)


def mix_columns(agg, weight):
    partial_terms = jnp.dot(agg, weight, preferred_element_type=jnp.float32)
    return lax.psum_scatter(partial_terms, "rep", scatter_dimension=1, tiled=True)


def widen(local):
    return lax.all_gather(local, "rep", axis=1, tiled=True)


def split_body(features, edge_tiles, sources, counts, w_first, w_second, cotangent):
    group_rows, slots, block, _ = edge_tiles.shape
    height, width = features.shape
    live = jnp.arange(slots, dtype=jnp.int32)[None, :] < counts[:, None]
    live_tiles = edge_tiles * live[:, :, None, None].astype(edge_tiles.dtype)
    scale = 1.0 / math.sqrt(height * lax.axis_size("row"))
    agg_first = aggregate(features, live_tiles, sources)
    pre_first = mix_columns(agg_first, w_first)
    hidden = jax.nn.silu(pre_first).astype(jnp.bfloat16)
    agg_second = aggregate(hidden, live_tiles, sources)
    embeddings = mix_columns(agg_second, w_second).astype(jnp.bfloat16)
    full_cotangent = widen(cotangent)
    second_part = jnp.dot(agg_second.T, full_cotangent, preferred_element_type=jnp.float32) * scale
    back_agg = jnp.dot(full_cotangent, w_second.T, preferred_element_type=jnp.float32).astype(
        jnp.bfloat16
    )
    contrib = spread_back(back_agg, live_tiles)
    flat_sources = sources.reshape(-1)
    flat_contrib = contrib.reshape(group_rows * slots, block * width)
    count = height * lax.axis_size("row")
    wanted = count // block
    inside = (flat_sources >= 0) & (flat_sources < wanted)
    target = jnp.where(inside, flat_sources, wanted)
    summed = jax.ops.segment_sum(flat_contrib, target, num_segments=wanted + 1)
    back_hidden = lax.psum_scatter(
        summed[:wanted].reshape(count, width), "row", scatter_dimension=0, tiled=True
    )
    back_pre = (back_hidden * silu_slope(pre_first)).astype(jnp.bfloat16)
    first_part = jnp.dot(agg_first.T, widen(back_pre), preferred_element_type=jnp.float32) * scale
    grad_second, grad_first = lax.psum((second_part, first_part), "row")
    return (embeddings, grad_first, grad_second)


def dot(a, b, contract):
    return lax.dot_general(a, b, (contract, ((), ())), preferred_element_type=F32)


def pack_kernel(
    chips, parts, sources_ref, counts_ref, feat_ref, cot_ref, tiles_ref, w1_ref, w2_ref, *outs
):
    for_chips, for_reps, row_ref, sems = outs
    _, slots, block, _ = tiles_ref.shape
    width = feat_ref.shape[1]
    core = lax.rem(lax.axis_index("row"), CORES)
    moves = [
        (feat_ref, for_reps.at[0, :, pl.ds(0, width)]),
        (cot_ref, for_reps.at[0, :, pl.ds(width, width)]),
    ]
    copies = [pltpu.make_async_copy(*move, sems.at[slots + n]) for n, move in enumerate(moves)]
    for copy in copies:
        copy.start()
    step = for_reps.shape[2]
    halves = w1_ref.shape[1] // step

    def weight_copy(ref, n):
        lanes = pl.ds(n * step, step)
        return pltpu.make_async_copy(ref.at[:, lanes], for_reps.at[1 + n], sems.at[slots + 2 + n])

    for c, ref in enumerate((w1_ref, w2_ref)):
        for n in range(halves):
            pl.when(core == c)(lambda ref=ref, n=n: weight_copy(ref, n).start())
    row_ref[...] = jnp.zeros_like(row_ref)

    def tile_copy(k):
        source = sources_ref[0, k]
        position = lax.rem(source, CORES) * chips + lax.div(source, CORES)
        columns = pl.ds(pl.multiple_of(position * block, block), block)
        return pltpu.make_async_copy(tiles_ref.at[0, k], row_ref.at[:, columns], sems.at[k])

    for k in range(slots):
        pl.when(k < counts_ref[0])(lambda k=k: tile_copy(k).start())
    for copy in copies:
        copy.wait()
    for_chips[0] = for_reps[0]
    for k in range(slots):
        pl.when(k < counts_ref[0])(lambda k=k: tile_copy(k).wait())
    share = parts * block
    start = pl.multiple_of(lax.axis_index("rep") * share, share)
    for_chips[1] = row_ref[:, pl.ds(start, share)]
    for c, ref in enumerate((w1_ref, w2_ref)):
        for n in range(halves):
            pl.when(core == c)(lambda ref=ref, n=n: weight_copy(ref, n).wait())


def join_kernel(*refs):
    out_ref = refs[-1]
    size = refs[0].shape[0]
    for n, ref in enumerate(refs[:-1]):
        out_ref[pl.ds(n * size, size)] = ref[...]


def layers_kernel(chips, reps, scale, *refs):
    count = CORES * reps
    locals_, nears, fars, refs = (*(refs[n * count :][:count] for n in range(3)), refs[3 * count :])
    own_rows, refs = refs[:CORES], refs[CORES:]
    emb_ref, gf_ref, gs_ref, a_s, f_s, c_s, w_s, af_s, hid_s, slope_s, ba_s = refs
    row, rep = lax.axis_index("row"), lax.axis_index("rep")
    core, chip = lax.rem(row, CORES), lax.div(row, CORES)
    height, width = emb_ref.shape
    nodes, wide = f_s.shape
    share = nodes // reps

    def at(index, size):
        return pl.ds(pl.multiple_of(index * size, size), size)

    for d in range(reps):
        q = rep ^ d
        for dc in range(CORES):
            n, c = dc * reps + d, core ^ dc

            def place(ref, first, dz, q=q, c=c):
                rows = at(c * chips + (chip ^ dz), height)
                f_s[rows, at(q, width)] = ref[first, :, :width]
                c_s[rows, at(q, width)] = ref[first, :, width:]
                if dz:
                    a_s[rows, at(q, share)] = ref[first + 1]

            place(locals_[n], 0, 0)
            place(nears[n], 0, 1)
            for dz in range(2, chips):
                place(fars[n], 2 * (dz - 2), dz)
            step = locals_[n].shape[2]
            for h in range(wide // step):
                w_s[c, at(q, width), h * step : (h + 1) * step] = locals_[n][1 + h]
    for dc in range(CORES):
        a_s[at((core ^ dc) * chips + chip, height)] = own_rows[dc][...]

    my_cols = at(rep, width)
    step = 2 * height

    def forward(i, _):
        rows = at(i, step)
        agg = dot(a_s[rows, :], f_s[...], ((1,), (0,))).astype(BF16)
        af_s[rows, :] = agg
        pre = dot(agg, w_s[0], ((1,), (0,)))
        sig = jax.nn.sigmoid(pre)
        hid_s[rows, :] = (pre * sig).astype(BF16)
        slope_s[rows, :] = sig * (1.0 + pre * (1.0 - sig))
        ba_s[rows, :] = dot(c_s[rows, :], w_s[1], ((1,), (1,))).astype(BF16)
        return 0

    lax.fori_loop(0, nodes // step, forward, 0)

    gf_ref[...] = jnp.zeros_like(gf_ref)
    gs_ref[...] = jnp.zeros_like(gs_ref)

    def backward(i, _):
        rows = at(i, step)
        back_hidden = dot(a_s[:, rows], ba_s[...], ((0,), (0,)))
        back_pre = (back_hidden * slope_s[rows, :]).astype(BF16)
        gf_ref[...] += dot(af_s[rows, my_cols], back_pre, ((0,), (0,)))
        agg = dot(a_s[rows, :], hid_s[:, my_cols], ((1,), (0,))).astype(BF16)
        gs_ref[...] += dot(agg, c_s[rows, :], ((0,), (0,)))
        return 0

    lax.fori_loop(0, nodes // step, backward, 0)
    gf_ref[...] = gf_ref[...] * scale
    gs_ref[...] = gs_ref[...] * scale

    agg_mine = dot(a_s[at(core * chips + chip, height), :], hid_s[...], ((1,), (0,))).astype(BF16)
    emb_ref[...] = dot(agg_mine, w_s[1, :, my_cols], ((1,), (0,))).astype(BF16)


def whole_body(features, edge_tiles, sources, counts, w_first, w_second, cotangent):
    _, slots, block, _ = edge_tiles.shape
    height, width = features.shape
    rows, reps = lax.axis_size("row"), lax.axis_size("rep")
    chips = rows // CORES
    nodes = height * rows
    share = nodes // reps
    wide = width * reps
    vmem = pl.BlockSpec(memory_space=pltpu.VMEM)
    smem = pl.BlockSpec(memory_space=pltpu.SMEM)
    hbm = pl.BlockSpec(memory_space=pltpu.HBM)
    shape = jax.ShapeDtypeStruct
    limit = pltpu.CompilerParams(vmem_limit_bytes=24 * 2**20)

    in_hbm = [
        pltpu.with_memory_space_constraint(v, pltpu.HBM)
        for v in (features, cotangent, edge_tiles, w_first, w_second)
    ]
    for_chips, for_reps, my_row = pl.pallas_call(
        functools.partial(pack_kernel, chips, share // block),
        out_shape=(
            shape((2, height, share), BF16),
            shape((1 + wide // share, height, share), BF16),
            shape((height, nodes), BF16),
        ),
        in_specs=[smem, smem] + [hbm] * 5,
        out_specs=(vmem,) * 3,
        scratch_shapes=[pltpu.SemaphoreType.DMA((slots + 2 + wide // share,))],
        compiler_params=limit,
        name="pack",
    )(sources, counts, *in_hbm)

    def swap(value, axis, size, d):
        return lax.ppermute(value, axis, [(i, i ^ d) for i in range(size)])

    def spread(value):
        far_first = range(reps - 1, 0, -1)
        got = {d: swap(value, "rep", reps, d) for d in far_first}
        values = [value] + [got[d] for d in range(1, reps)]
        return values + [swap(v, "row", rows, 1) for v in values]

    near, *far = [swap(for_chips, "row", rows, CORES * d) for d in range(1, chips)]
    joined = pl.pallas_call(
        join_kernel,
        out_shape=shape((2 * (chips - 2), height, share), BF16),
        in_specs=[vmem] * (chips - 2),
        out_specs=vmem,
        compiler_params=limit,
        name="join",
    )(*far)
    pieces = spread(for_reps) + spread(near) + spread(joined)
    own_rows = [my_row, swap(my_row, "row", rows, 1)]

    return tuple(
        pl.pallas_call(
            functools.partial(layers_kernel, chips, reps, 1.0 / math.sqrt(nodes)),
            out_shape=(
                shape((height, width), BF16),
                shape((width, wide), F32),
                shape((width, wide), F32),
            ),
            in_specs=[vmem] * (3 * CORES * reps + CORES),
            out_specs=(vmem, vmem, vmem),
            scratch_shapes=[
                pltpu.VMEM((nodes, nodes), BF16),
                pltpu.VMEM((nodes, wide), BF16),
                pltpu.VMEM((nodes, wide), BF16),
                pltpu.VMEM((2, wide, wide), BF16),
                pltpu.VMEM((nodes, wide), BF16),
                pltpu.VMEM((nodes, wide), BF16),
                pltpu.VMEM((nodes, wide), F32),
                pltpu.VMEM((nodes, wide), BF16),
            ],
            compiler_params=limit,
            name="layers",
        )(*pieces, *own_rows)
    )


def fits_whole(features, edge_tiles, rows, reps):
    nodes, wide = features.shape
    block = edge_tiles.shape[2]
    powers = all(n & (n - 1) == 0 for n in (rows, reps))
    held = 2 * (nodes * nodes + 2 * nodes * wide + 2 * wide * wide)
    width, share = wide // reps, nodes // reps
    return (
        held <= REPLICATED_BYTES
        and powers
        and rows % CORES == 0
        and nodes // rows == block == width
        and share % block == 0
        and share == 2 * width
        and wide % share == 0
        and rows // CORES > 2
    )


def solution(mesh):
    placed = (
        P("row", "rep"),
        P("row", None, None, None),
        P("row", None),
        P("row"),
        P("rep", None),
        P("rep", None),
        P("row", "rep"),
    )

    rows, reps = mesh.shape["row"], mesh.shape["rep"]
    outs = (P("row", "rep"), P("rep", None), P("rep", None))

    def run(features, edge_tiles, *rest):
        whole = fits_whole(features, edge_tiles, rows, reps)

        def body(*args):
            return (whole_body if whole else split_body)(*args)

        step = jax.shard_map(body, mesh=mesh, in_specs=placed, out_specs=outs, check_vma=False)
        return step(features, edge_tiles, *rest)

    return run
```

```python
import functools
import math

import jax
import jax.numpy as jnp
from jax import lax
from jax.experimental import pallas as pl
from jax.experimental.pallas import tpu as pltpu
from jax.sharding import PartitionSpec as P

BF16 = jnp.bfloat16
F32 = jnp.float32
CORES = 2
REPLICATED_BYTES = 16 * 2**20


def silu_slope(value):
    sig = jax.nn.sigmoid(value)
    return sig * (1.0 + value * (1.0 - sig))


def gather_blocks(local, block):
    height, width = local.shape
    packed = local.reshape(height * width // 128, 128)
    whole = lax.all_gather(packed, "row", axis=0, tiled=True)
    return whole.reshape(-1, block, width)


def aggregate(local, live_tiles, sources):
    height, width = local.shape
    _, _, block, _ = live_tiles.shape
    blocks = gather_blocks(local, block)
    total = jnp.einsum(
        "bkij,bkjf->bif", live_tiles, blocks[sources], preferred_element_type=jnp.float32
    )
    return total.reshape(height, width).astype(jnp.bfloat16)


def spread_back(back_agg, live_tiles):
    group_rows, _, block, _ = live_tiles.shape
    width = back_agg.shape[1]
    block_rows = back_agg.reshape(group_rows, block, width)
    return jnp.einsum("bkij,bif->bkjf", live_tiles, block_rows, preferred_element_type=jnp.float32)


def mix_columns(agg, weight):
    partial_terms = jnp.dot(agg, weight, preferred_element_type=jnp.float32)
    return lax.psum_scatter(partial_terms, "rep", scatter_dimension=1, tiled=True)


def widen(local):
    return lax.all_gather(local, "rep", axis=1, tiled=True)


def split_body(features, edge_tiles, sources, counts, w_first, w_second, cotangent):
    group_rows, slots, block, _ = edge_tiles.shape
    height, width = features.shape
    live = jnp.arange(slots, dtype=jnp.int32)[None, :] < counts[:, None]
    live_tiles = edge_tiles * live[:, :, None, None].astype(edge_tiles.dtype)
    scale = 1.0 / math.sqrt(height * lax.axis_size("row"))
    agg_first = aggregate(features, live_tiles, sources)
    pre_first = mix_columns(agg_first, w_first)
    hidden = jax.nn.silu(pre_first).astype(jnp.bfloat16)
    agg_second = aggregate(hidden, live_tiles, sources)
    embeddings = mix_columns(agg_second, w_second).astype(jnp.bfloat16)
    full_cotangent = widen(cotangent)
    second_part = jnp.dot(agg_second.T, full_cotangent, preferred_element_type=jnp.float32) * scale
    back_agg = jnp.dot(full_cotangent, w_second.T, preferred_element_type=jnp.float32).astype(
        jnp.bfloat16
    )
    contrib = spread_back(back_agg, live_tiles)
    flat_sources = sources.reshape(-1)
    flat_contrib = contrib.reshape(group_rows * slots, block * width)
    count = height * lax.axis_size("row")
    wanted = count // block
    inside = (flat_sources >= 0) & (flat_sources < wanted)
    target = jnp.where(inside, flat_sources, wanted)
    summed = jax.ops.segment_sum(flat_contrib, target, num_segments=wanted + 1)
    back_hidden = lax.psum_scatter(
        summed[:wanted].reshape(count, width), "row", scatter_dimension=0, tiled=True
    )
    back_pre = (back_hidden * silu_slope(pre_first)).astype(jnp.bfloat16)
    first_part = jnp.dot(agg_first.T, widen(back_pre), preferred_element_type=jnp.float32) * scale
    grad_second, grad_first = lax.psum((second_part, first_part), "row")
    return (embeddings, grad_first, grad_second)


def dot(a, b, contract):
    return lax.dot_general(a, b, (contract, ((), ())), preferred_element_type=F32)


def pack_kernel(
    chips, parts, counts_ref, sources_hbm, feat_ref, cot_ref, tiles_ref, w1_ref, w2_ref, *outs
):
    for_chips, for_reps, for_next, sems, sources_ref, index_sem = outs
    index_copy = pltpu.make_async_copy(sources_hbm, sources_ref, index_sem)
    index_copy.start()
    _, slots, block, _ = tiles_ref.shape
    width = feat_ref.shape[1]
    core = lax.rem(lax.axis_index("row"), CORES)
    moves = [
        (feat_ref, for_reps.at[0, :, pl.ds(0, width)]),
        (cot_ref, for_reps.at[0, :, pl.ds(width, width)]),
    ]
    copies = [pltpu.make_async_copy(*move, sems.at[slots + n]) for n, move in enumerate(moves)]
    for copy in copies:
        copy.start()
    step = for_reps.shape[2]

    def weight_copy(ref, n):
        lanes = pl.ds(n * step, step)
        return pltpu.make_async_copy(ref.at[:, lanes], for_reps.at[1 + n], sems.at[slots + 2 + n])

    for c, ref in enumerate((w1_ref, w2_ref)):
        for n in range(2):
            pl.when(core == c)(lambda ref=ref, n=n: weight_copy(ref, n).start())
    for_next[1:] = jnp.zeros_like(for_next[1:])
    index_copy.wait()

    def tile_copy(k):
        source = sources_ref[0, k]
        position = lax.rem(source, CORES) * chips + lax.div(source, CORES)
        columns = pl.ds(pl.multiple_of(lax.rem(position, parts) * block, block), block)
        target = for_next.at[1 + lax.div(position, parts), :, columns]
        return pltpu.make_async_copy(tiles_ref.at[0, k], target, sems.at[k])

    for k in range(slots):
        pl.when(k < counts_ref[0])(lambda k=k: tile_copy(k).start())
    for copy in copies:
        copy.wait()
    for_chips[0] = for_reps[0]
    for_next[0] = for_reps[0]
    for k in range(slots):
        pl.when(k < counts_ref[0])(lambda k=k: tile_copy(k).wait())
    for_chips[1] = for_next[1 + lax.axis_index("rep")]
    for c, ref in enumerate((w1_ref, w2_ref)):
        for n in range(2):
            pl.when(core == c)(lambda ref=ref, n=n: weight_copy(ref, n).wait())


def at(index, size, start=0):
    return pl.ds(pl.multiple_of(start + index * size, size), size)


def place_features(out_ref, rows, rep, blocks):
    reps = len(blocks)
    width = blocks[0].shape[1] // 2
    for d, block in enumerate(blocks):
        out_ref[rows, at(rep ^ d, width)] = block[:, :width]
        out_ref[rows, at(rep ^ d, width, width * reps)] = block[:, width:]


def place_adjacency(out_ref, for_next):
    share = for_next.shape[2]
    count = for_next.shape[0] - 1
    start = out_ref.shape[1] - count * share
    for j in range(count):
        out_ref[:, start + j * share : start + (j + 1) * share] = for_next[1 + j]


def own_kernel(*refs):
    *own, for_next, rows_ref, weight_ref, peers_ref = refs
    rep = lax.axis_index("rep")
    _, height, share = for_next.shape
    everything = pl.ds(0, height)
    place_features(rows_ref, everything, rep, [ref[0] for ref in own])
    place_adjacency(rows_ref, for_next)
    width = weight_ref.shape[0] // len(own)
    for d, ref in enumerate(own):
        for n in range(2):
            weight_ref[at(rep ^ d, width), n * share : (n + 1) * share] = ref[1 + n]
        if d:
            peers_ref[d - 1] = ref[0]


def next_kernel(from_next, peers, rows_ref):
    rep = lax.axis_index("rep")
    everything = pl.ds(0, from_next.shape[1])
    blocks = [from_next[0]] + [peers[d] for d in range(peers.shape[0])]
    place_features(rows_ref, everything, rep, blocks)
    place_adjacency(rows_ref, from_next)


def far_kernel(*refs):
    *blocks, out_ref = refs
    reps = len(blocks) // 2
    rep = lax.axis_index("rep")
    half = lax.rem(lax.div(lax.axis_index("row"), CORES), 2)
    _, height, share = blocks[0].shape
    for parity, chunk in ((half, blocks[:reps]), (1 - half, blocks[reps:])):
        rows = at(parity, height)
        place_features(out_ref, rows, rep, [ref[0] for ref in chunk])
        for d, ref in enumerate(chunk):
            out_ref[rows, at(rep ^ d, share, share * reps)] = ref[1]


def place_of(b):
    row = lax.axis_index("row")
    core, chip = lax.rem(row, CORES), lax.div(row, CORES)
    dh, dc = divmod(b, CORES)
    return (core ^ dc) * 2 + (lax.div(chip, 2) ^ dh)


def parts_of(bundle, wide, step):
    return (
        bundle[:, :wide],
        bundle[:, wide : 2 * wide],
        lambda b: bundle[:, at(place_of(b), step, 2 * wide)],
    )


def total_of(terms):
    total = None
    for term in terms:
        total = term if total is None else total + term
    return total


def back_aggregates(cotangent, weight):
    return dot(cotangent, weight, ((1,), (1,))).astype(BF16)


def early_kernel(*refs):
    own_rows, next_rows, weights, refs = refs[:2], refs[2:4], refs[4:6], refs[6:]
    first_bundle, second_bundle, w_ref, back_ref, agg_ref, ba_s = refs
    bundles = first_bundle, second_bundle
    row = lax.axis_index("row")
    core, half = lax.rem(row, CORES), lax.rem(lax.div(row, CORES), 2)
    height = own_rows[0].shape[0]
    wide = w_ref.shape[1]
    for c in range(CORES):
        bundles[c][at(half, height), :] = own_rows[c][...]
        bundles[c][at(1 - half, height), :] = next_rows[c][...]
        w_ref[core ^ c] = weights[c][...]
    parts = [parts_of(bundle, wide, 2 * height) for bundle in bundles]
    for k, (_, cotangent, _) in enumerate(parts):
        ba_s[k] = back_aggregates(cotangent[...], w_ref[1])
    for b in range(2 * CORES):
        terms = (dot(a(b), ba_s[k], ((0,), (0,))) for k, (_, _, a) in enumerate(parts))
        back_ref[b] = total_of(terms)
    for b, (_, _, a) in enumerate(parts):
        terms = (dot(a(k), feats, ((1,), (0,))) for k, (feats, _, _) in enumerate(parts))
        agg_ref[b] = total_of(terms)


def middle_kernel(*refs):
    bundles, (w_ref, back_in, agg_in), (back_ref, agg_ref) = refs[:3], refs[3:6], refs[6:]
    step = bundles[0].shape[0]
    parts = [parts_of(bundle, w_ref.shape[1], step) for bundle in bundles]
    feats, cotangent, a = parts[CORES]
    back_agg = back_aggregates(cotangent, w_ref[1])
    for b in range(2 * CORES):
        back_ref[b] = back_in[b] + dot(a(b), back_agg, ((0,), (0,)))
    for b in range(CORES):
        agg_ref[b] = agg_in[b] + dot(parts[b][2](CORES), feats, ((1,), (0,)))
    agg_ref[CORES] = total_of(dot(a(k), parts[k][0], ((1,), (0,))) for k in range(CORES + 1))


def layers_kernel(reps, scale, *refs):
    bundles, (w_ref, back_ref, early_agg_ref), refs = refs[:4], refs[4:7], refs[7:]
    emb_ref, gf_ref, gs_ref, af_s, hid_s, slope_s = refs
    row, rep = lax.axis_index("row"), lax.axis_index("rep")
    chip = lax.div(row, CORES)
    height, width = emb_ref.shape
    wide = width * reps
    step = 2 * height
    count = len(bundles)
    my_cols = at(rep, width)
    parts = [parts_of(bundle, wide, step) for bundle in bundles]

    last = count - 1
    back_agg = back_aggregates(parts[last][1], w_ref[1])
    for b in range(count):
        a = parts[b][2]
        if b < last:
            total = early_agg_ref[b] + dot(a(last), parts[last][0], ((1,), (0,)))
        else:
            total = total_of(dot(a(k), parts[k][0], ((1,), (0,))) for k in range(count))
        agg = total.astype(BF16)
        af_s[b] = agg
        pre = dot(agg, w_ref[0], ((1,), (0,)))
        sig = jax.nn.sigmoid(pre)
        hid_s[b] = (pre * sig).astype(BF16)
        slope_s[b] = sig * (1.0 + pre * (1.0 - sig))

    for b in range(count):
        _, cotangent, a = parts[b]
        back_hidden = back_ref[b] + dot(parts[last][2](b), back_agg, ((0,), (0,)))
        back_pre = (back_hidden * slope_s[b]).astype(BF16)
        agg = total_of(dot(a(k), hid_s[k, :, my_cols], ((1,), (0,))) for k in range(count))
        gf = dot(af_s[b, :, my_cols], back_pre, ((0,), (0,)))
        gs = dot(agg.astype(BF16), cotangent, ((0,), (0,)))
        gf_ref[...] = gf if b == 0 else gf_ref[...] + gf
        gs_ref[...] = gs if b == 0 else gs_ref[...] + gs
    gf_ref[...] = gf_ref[...] * scale
    gs_ref[...] = gs_ref[...] * scale

    mine = at(lax.rem(chip, 2), height)
    agg = total_of(
        dot(bundles[0][mine, at(place_of(k), step, 2 * wide)], hid_s[k], ((1,), (0,)))
        for k in range(count)
    )
    emb_ref[...] = dot(agg.astype(BF16), w_ref[1, :, my_cols], ((1,), (0,))).astype(BF16)


def whole_body(features, edge_tiles, sources, counts, w_first, w_second, cotangent):
    _, slots, block, _ = edge_tiles.shape
    height, width = features.shape
    rows, reps = lax.axis_size("row"), lax.axis_size("rep")
    chips = rows // CORES
    nodes = height * rows
    share = nodes // reps
    wide = width * reps
    vmem = pl.BlockSpec(memory_space=pltpu.VMEM)
    hbm = pl.BlockSpec(memory_space=pltpu.HBM)
    shape = jax.ShapeDtypeStruct
    step = 2 * height
    rows_shape = shape((height, 2 * wide + nodes), BF16)
    bundle_shape = shape((step, 2 * wide + nodes), BF16)
    limit = pltpu.CompilerParams(vmem_limit_bytes=24 * 2**20)

    in_hbm = [
        pltpu.with_memory_space_constraint(v, pltpu.HBM)
        for v in (sources, features, cotangent, edge_tiles, w_first, w_second)
    ]
    for_chips, for_reps, for_next = pl.pallas_call(
        functools.partial(pack_kernel, chips, share // block),
        out_shape=(
            shape((2, height, share), BF16),
            shape((3, height, share), BF16),
            shape((1 + reps, height, share), BF16),
        ),
        in_specs=[pl.BlockSpec(memory_space=pltpu.SMEM)] + [hbm] * 6,
        out_specs=(vmem,) * 3,
        scratch_shapes=[
            pltpu.SemaphoreType.DMA((slots + 4,)),
            pltpu.SMEM(sources.shape, sources.dtype),
            pltpu.SemaphoreType.DMA,
        ],
        compiler_params=limit,
        name="pack",
    )(counts, *in_hbm)

    def swap(value, axis, size, d):
        return lax.ppermute(value, axis, [(i, i ^ d) for i in range(size)])

    def spread(value, name):
        values = [value]
        for d in range(1, reps):
            via, hop = hop_of(name, d)
            values.append(swap(values[via], "rep", reps, hop))
        return values

    def local(kernel, outs, *operands, scratch=()):
        return pl.pallas_call(
            kernel,
            out_shape=outs,
            in_specs=[vmem] * len(operands),
            out_specs=(vmem,) * len(outs),
            scratch_shapes=scratch,
            compiler_params=limit,
        )(*operands)

    def pair(value):
        return value, swap(value, "row", rows, 1)

    third = swap(for_chips, "row", rows, CORES * 3)
    second = swap(for_chips, "row", rows, CORES * 2)
    from_next = swap(for_next, "row", rows, CORES)
    own, third, second = spread(for_reps, "own"), spread(third, "third"), spread(second, "second")

    outs = (rows_shape, shape((wide, wide), BF16), shape((reps - 1, height, share), BF16))
    own_rows, weight, peers = local(own_kernel, outs, *own, for_next)
    peers = swap(peers, "row", rows, CORES)
    (next_rows,) = local(next_kernel, (rows_shape,), from_next, peers)
    (far_bundle,) = local(far_kernel, (bundle_shape,), *second, *third)
    outs = (
        *(bundle_shape, bundle_shape),
        shape((2, wide, wide), BF16),
        shape((2 * CORES, step, wide), F32),
        shape((CORES, step, wide), F32),
    )
    *near_bundles, weights, back, agg = local(
        early_kernel,
        outs,
        *pair(own_rows),
        *pair(next_rows),
        *pair(weight),
        scratch=[pltpu.VMEM((CORES, step, wide), BF16)],
    )
    far_pair = pair(far_bundle)
    back, agg = local(
        middle_kernel,
        (shape((2 * CORES, step, wide), F32), shape((CORES + 1, step, wide), F32)),
        *near_bundles,
        far_bundle,
        *(weights, back, agg),
    )
    outs = (shape((height, width), BF16), shape((width, wide), F32), shape((width, wide), F32))
    return local(
        functools.partial(layers_kernel, reps, 1.0 / math.sqrt(nodes)),
        outs,
        *near_bundles,
        *far_pair,
        *(weights, back, agg),
        scratch=[
            pltpu.VMEM((2 * CORES, step, wide), BF16),
            pltpu.VMEM((2 * CORES, step, wide), BF16),
            pltpu.VMEM((2 * CORES, step, wide), F32),
        ],
    )


RELAYED = {}


def hop_of(name, d):
    hop = RELAYED.get(name, 0) & d
    return (d ^ hop, hop) if hop and hop != d else (0, d)


def fits_whole(features, edge_tiles, rows, reps):
    nodes, wide = features.shape
    block = edge_tiles.shape[2]
    powers = all(n & (n - 1) == 0 for n in (rows, reps))
    held = 2 * (nodes * nodes + 2 * nodes * wide + 2 * wide * wide)
    width, share = wide // reps, nodes // reps
    return (
        held <= REPLICATED_BYTES
        and powers
        and rows % CORES == 0
        and nodes // rows == block == width
        and share % block == 0
        and share == 2 * width
        and wide == 2 * share
        and rows == 4 * CORES
    )


def solution(mesh):
    placed = (
        P("row", "rep"),
        P("row", None, None, None),
        P("row", None),
        P("row"),
        P("rep", None),
        P("rep", None),
        P("row", "rep"),
    )

    rows, reps = mesh.shape["row"], mesh.shape["rep"]
    outs = (P("row", "rep"), P("rep", None), P("rep", None))

    def run(features, edge_tiles, *rest):
        whole = fits_whole(features, edge_tiles, rows, reps)

        def body(*args):
            return (whole_body if whole else split_body)(*args)

        step = jax.shard_map(body, mesh=mesh, in_specs=placed, out_specs=outs, check_vma=False)
        return step(features, edge_tiles, *rest)

    return run
```

```python
import functools
import math

import jax
import jax.numpy as jnp
from jax import lax
from jax.experimental import pallas as pl
from jax.experimental.pallas import tpu as pltpu
from jax.sharding import PartitionSpec as P

BF16 = jnp.bfloat16
F32 = jnp.float32
CORES = 2
REPLICATED_BYTES = 16 * 2**20


def silu_slope(value):
    sig = jax.nn.sigmoid(value)
    return sig * (1.0 + value * (1.0 - sig))


def gather_blocks(local, block):
    height, width = local.shape
    packed = local.reshape(height * width // 128, 128)
    whole = lax.all_gather(packed, "row", axis=0, tiled=True)
    return whole.reshape(-1, block, width)


def aggregate(local, live_tiles, sources):
    height, width = local.shape
    _, _, block, _ = live_tiles.shape
    blocks = gather_blocks(local, block)
    total = jnp.einsum(
        "bkij,bkjf->bif", live_tiles, blocks[sources], preferred_element_type=jnp.float32
    )
    return total.reshape(height, width).astype(jnp.bfloat16)


def spread_back(back_agg, live_tiles):
    group_rows, _, block, _ = live_tiles.shape
    width = back_agg.shape[1]
    block_rows = back_agg.reshape(group_rows, block, width)
    return jnp.einsum("bkij,bif->bkjf", live_tiles, block_rows, preferred_element_type=jnp.float32)


def mix_columns(agg, weight):
    partial_terms = jnp.dot(agg, weight, preferred_element_type=jnp.float32)
    return lax.psum_scatter(partial_terms, "rep", scatter_dimension=1, tiled=True)


def widen(local):
    return lax.all_gather(local, "rep", axis=1, tiled=True)


def split_body(features, edge_tiles, sources, counts, w_first, w_second, cotangent):
    group_rows, slots, block, _ = edge_tiles.shape
    height, width = features.shape
    live = jnp.arange(slots, dtype=jnp.int32)[None, :] < counts[:, None]
    live_tiles = edge_tiles * live[:, :, None, None].astype(edge_tiles.dtype)
    scale = 1.0 / math.sqrt(height * lax.axis_size("row"))
    agg_first = aggregate(features, live_tiles, sources)
    pre_first = mix_columns(agg_first, w_first)
    hidden = jax.nn.silu(pre_first).astype(jnp.bfloat16)
    agg_second = aggregate(hidden, live_tiles, sources)
    embeddings = mix_columns(agg_second, w_second).astype(jnp.bfloat16)
    full_cotangent = widen(cotangent)
    second_part = jnp.dot(agg_second.T, full_cotangent, preferred_element_type=jnp.float32) * scale
    back_agg = jnp.dot(full_cotangent, w_second.T, preferred_element_type=jnp.float32).astype(
        jnp.bfloat16
    )
    contrib = spread_back(back_agg, live_tiles)
    flat_sources = sources.reshape(-1)
    flat_contrib = contrib.reshape(group_rows * slots, block * width)
    count = height * lax.axis_size("row")
    wanted = count // block
    inside = (flat_sources >= 0) & (flat_sources < wanted)
    target = jnp.where(inside, flat_sources, wanted)
    summed = jax.ops.segment_sum(flat_contrib, target, num_segments=wanted + 1)
    back_hidden = lax.psum_scatter(
        summed[:wanted].reshape(count, width), "row", scatter_dimension=0, tiled=True
    )
    back_pre = (back_hidden * silu_slope(pre_first)).astype(jnp.bfloat16)
    first_part = jnp.dot(agg_first.T, widen(back_pre), preferred_element_type=jnp.float32) * scale
    grad_second, grad_first = lax.psum((second_part, first_part), "row")
    return (embeddings, grad_first, grad_second)


def dot(a, b, contract):
    return lax.dot_general(a, b, (contract, ((), ())), preferred_element_type=F32)


def pack_kernel(
    chips, parts, counts_ref, sources_hbm, feat_ref, cot_ref, tiles_ref, w1_ref, w2_ref, *outs
):
    for_chips, for_reps, for_next, sems, sources_ref, index_sem = outs
    index_copy = pltpu.make_async_copy(sources_hbm, sources_ref, index_sem)
    index_copy.start()
    _, slots, block, _ = tiles_ref.shape
    width = feat_ref.shape[1]
    core = lax.rem(lax.axis_index("row"), CORES)
    moves = [
        (feat_ref, for_reps.at[0, :, pl.ds(0, width)]),
        (cot_ref, for_reps.at[0, :, pl.ds(width, width)]),
    ]
    copies = [pltpu.make_async_copy(*move, sems.at[slots + n]) for n, move in enumerate(moves)]
    for copy in copies:
        copy.start()
    step = for_reps.shape[2]

    def weight_copy(ref, n):
        lanes = pl.ds(n * step, step)
        return pltpu.make_async_copy(ref.at[:, lanes], for_reps.at[1 + n], sems.at[slots + 2 + n])

    for c, ref in enumerate((w1_ref, w2_ref)):
        for n in range(2):
            pl.when(core == c)(lambda ref=ref, n=n: weight_copy(ref, n).start())
    for_next[1:] = jnp.zeros_like(for_next[1:])
    index_copy.wait()

    def tile_copy(k):
        source = sources_ref[0, k]
        position = lax.rem(source, CORES) * chips + lax.div(source, CORES)
        columns = pl.ds(pl.multiple_of(lax.rem(position, parts) * block, block), block)
        target = for_next.at[1 + lax.div(position, parts), :, columns]
        return pltpu.make_async_copy(tiles_ref.at[0, k], target, sems.at[k])

    for k in range(slots):
        pl.when(k < counts_ref[0])(lambda k=k: tile_copy(k).start())
    for copy in copies:
        copy.wait()
    for_chips[0] = for_reps[0]
    for_next[0] = for_reps[0]
    for k in range(slots):
        pl.when(k < counts_ref[0])(lambda k=k: tile_copy(k).wait())
    for_chips[1] = for_next[1 + lax.axis_index("rep")]
    for c, ref in enumerate((w1_ref, w2_ref)):
        for n in range(2):
            pl.when(core == c)(lambda ref=ref, n=n: weight_copy(ref, n).wait())


def at(index, size, start=0):
    return pl.ds(pl.multiple_of(start + index * size, size), size)


def place_features(out_ref, rows, rep, blocks):
    reps = len(blocks)
    width = blocks[0].shape[1] // 2
    for d, block in enumerate(blocks):
        out_ref[rows, at(rep ^ d, width)] = block[:, :width]
        out_ref[rows, at(rep ^ d, width, width * reps)] = block[:, width:]


def place_adjacency(out_ref, for_next):
    share = for_next.shape[2]
    count = for_next.shape[0] - 1
    start = out_ref.shape[1] - count * share
    for j in range(count):
        out_ref[:, start + j * share : start + (j + 1) * share] = for_next[1 + j]


def own_kernel(*refs):
    *own, for_next, rows_ref, weight_ref, peers_ref = refs
    rep = lax.axis_index("rep")
    _, height, share = for_next.shape
    everything = pl.ds(0, height)
    place_features(rows_ref, everything, rep, [ref[0] for ref in own])
    place_adjacency(rows_ref, for_next)
    width = weight_ref.shape[0] // len(own)
    for d, ref in enumerate(own):
        for n in range(2):
            weight_ref[at(rep ^ d, width), n * share : (n + 1) * share] = ref[1 + n]
        if d:
            peers_ref[d - 1] = ref[0]


def next_kernel(from_next, peers, rows_ref):
    rep = lax.axis_index("rep")
    everything = pl.ds(0, from_next.shape[1])
    blocks = [from_next[0]] + [peers[d] for d in range(peers.shape[0])]
    place_features(rows_ref, everything, rep, blocks)
    place_adjacency(rows_ref, from_next)


def far_kernel(*refs):
    *blocks, feats_ref, rest_ref = refs
    reps = len(blocks) // 2
    rep = lax.axis_index("rep")
    half = lax.rem(lax.div(lax.axis_index("row"), CORES), 2)
    _, height, share = blocks[0].shape
    width = share // 2
    for parity, chunk in ((half, blocks[:reps]), (1 - half, blocks[reps:])):
        rows = at(parity, height)
        for d, ref in enumerate(chunk):
            feats_ref[rows, at(rep ^ d, width)] = ref[0, :, :width]
            rest_ref[rows, at(rep ^ d, width)] = ref[0, :, width:]
            rest_ref[rows, at(rep ^ d, share, width * reps)] = ref[1]


def place_of(b):
    row = lax.axis_index("row")
    core, chip = lax.rem(row, CORES), lax.div(row, CORES)
    dh, dc = divmod(b, CORES)
    return (core ^ dc) * 2 + (lax.div(chip, 2) ^ dh)


def parts_of(bundle, wide, step):
    feats, rest, start = (*bundle, 0) if isinstance(bundle, tuple) else (bundle, bundle, wide)
    return (
        feats[:, :wide],
        rest[:, start : start + wide],
        lambda b: rest[:, at(place_of(b), step, start + wide)],
    )


def total_of(terms):
    total = None
    for term in terms:
        total = term if total is None else total + term
    return total


def back_aggregates(cotangent, weight):
    return dot(cotangent, weight, ((1,), (1,))).astype(BF16)


def early_kernel(*refs):
    own_rows, next_rows, weights, refs = refs[:2], refs[2:4], refs[4:6], refs[6:]
    first_bundle, second_bundle, w_ref, back_ref, agg_ref, ba_s = refs
    bundles = first_bundle, second_bundle
    row = lax.axis_index("row")
    core, half = lax.rem(row, CORES), lax.rem(lax.div(row, CORES), 2)
    height = own_rows[0].shape[0]
    wide = w_ref.shape[1]
    for c in range(CORES):
        bundles[c][at(half, height), :] = own_rows[c][...]
        bundles[c][at(1 - half, height), :] = next_rows[c][...]
        w_ref[core ^ c] = weights[c][...]
    parts = [parts_of(bundle, wide, 2 * height) for bundle in bundles]
    for k, (_, cotangent, _) in enumerate(parts):
        ba_s[k] = back_aggregates(cotangent, w_ref[1])
    for b in range(2 * CORES):
        terms = (dot(a(b), ba_s[k], ((0,), (0,))) for k, (_, _, a) in enumerate(parts))
        back_ref[b] = total_of(terms)
    for b, (_, _, a) in enumerate(parts):
        terms = (dot(a(k), feats, ((1,), (0,))) for k, (feats, _, _) in enumerate(parts))
        agg_ref[b] = total_of(terms)


def middle_kernel(*refs):
    first, second, *far, w_ref, back_in, agg_in, back_ref, agg_ref = refs
    bundles = first, second, tuple(far)
    step = first.shape[0]
    parts = [parts_of(bundle, w_ref.shape[1], step) for bundle in bundles]
    feats, cotangent, a = parts[CORES]
    back_agg = back_aggregates(cotangent, w_ref[1])
    for b in range(2 * CORES):
        back_ref[b] = back_in[b] + dot(a(b), back_agg, ((0,), (0,)))
    for b in range(CORES):
        agg_ref[b] = agg_in[b] + dot(parts[b][2](CORES), feats, ((1,), (0,)))
    agg_ref[CORES] = total_of(dot(a(k), parts[k][0], ((1,), (0,))) for k in range(CORES + 1))


def activate(total, weight, agg_ref, hidden_ref, slope_ref):
    agg = total.astype(BF16)
    agg_ref[...] = agg
    pre = dot(agg, weight, ((1,), (0,)))
    sig = jax.nn.sigmoid(pre)
    hidden_ref[...] = (pre * sig).astype(BF16)
    slope_ref[...] = sig * (1.0 + pre * (1.0 - sig))


def hidden_kernel(*refs):
    first, second, far_rest, feats, w_ref, agg_in, *outs = refs
    step, wide = feats.shape
    bundles = first, second, (None, far_rest)
    for b, bundle in enumerate(bundles):
        rest, start = (bundle[1], wide) if b == CORES else (bundle, 2 * wide)
        columns = rest[:, at(place_of(CORES + 1), step, start)]
        total = agg_in[b] + dot(columns, feats[...], ((1,), (0,)))
        activate(total, w_ref[0], *(out.at[b] for out in outs))


def layers_kernel(reps, scale, *refs):
    first, second, *far, w_ref, back_ref, early_agg, early_hidden, early_slope = refs[:11]
    emb_ref, gf_ref, gs_ref, last_agg, last_hidden, last_slope = refs[11:]
    bundles = first, second, tuple(far[:2]), tuple(far[2:])
    row, rep = lax.axis_index("row"), lax.axis_index("rep")
    chip = lax.div(row, CORES)
    height, width = emb_ref.shape
    wide = width * reps
    step = 2 * height
    count = len(bundles)
    last = count - 1
    my_cols = at(rep, width)
    parts = [parts_of(bundle, wide, step) for bundle in bundles]

    back_agg = back_aggregates(parts[last][1], w_ref[1])
    a = parts[last][2]
    total = total_of(dot(a(k), parts[k][0], ((1,), (0,))) for k in range(count))
    activate(total, w_ref[0], last_agg, last_hidden, last_slope)
    agg_first, hidden, slope = (
        [early.at[b] for b in range(last)] + [late]
        for early, late in (
            (early_agg, last_agg),
            (early_hidden, last_hidden),
            (early_slope, last_slope),
        )
    )

    for b in range(count):
        _, cotangent, a = parts[b]
        back_hidden = back_ref[b] + dot(parts[last][2](b), back_agg, ((0,), (0,)))
        back_pre = (back_hidden * slope[b][...]).astype(BF16)
        agg = total_of(dot(a(k), hidden[k][:, my_cols], ((1,), (0,))) for k in range(count))
        gf = dot(agg_first[b][:, my_cols], back_pre, ((0,), (0,)))
        gs = dot(agg.astype(BF16), cotangent, ((0,), (0,)))
        gf_ref[...] = gf if b == 0 else gf_ref[...] + gf
        gs_ref[...] = gs if b == 0 else gs_ref[...] + gs
    gf_ref[...] = gf_ref[...] * scale
    gs_ref[...] = gs_ref[...] * scale

    mine = at(lax.rem(chip, 2), height)
    agg = total_of(
        dot(first[mine, at(place_of(k), step, 2 * wide)], hidden[k][...], ((1,), (0,)))
        for k in range(count)
    )
    emb_ref[...] = dot(agg.astype(BF16), w_ref[1, :, my_cols], ((1,), (0,))).astype(BF16)


def whole_body(features, edge_tiles, sources, counts, w_first, w_second, cotangent):
    _, slots, block, _ = edge_tiles.shape
    height, width = features.shape
    rows, reps = lax.axis_size("row"), lax.axis_size("rep")
    chips = rows // CORES
    nodes = height * rows
    share = nodes // reps
    wide = width * reps
    vmem = pl.BlockSpec(memory_space=pltpu.VMEM)
    hbm = pl.BlockSpec(memory_space=pltpu.HBM)
    shape = jax.ShapeDtypeStruct
    step = 2 * height
    rows_shape = shape((height, 2 * wide + nodes), BF16)
    bundle_shape = shape((step, 2 * wide + nodes), BF16)
    limit = pltpu.CompilerParams(vmem_limit_bytes=24 * 2**20)

    in_hbm = [
        pltpu.with_memory_space_constraint(v, pltpu.HBM)
        for v in (sources, features, cotangent, edge_tiles, w_first, w_second)
    ]
    for_chips, for_reps, for_next = pl.pallas_call(
        functools.partial(pack_kernel, chips, share // block),
        out_shape=(
            shape((2, height, share), BF16),
            shape((3, height, share), BF16),
            shape((1 + reps, height, share), BF16),
        ),
        in_specs=[pl.BlockSpec(memory_space=pltpu.SMEM)] + [hbm] * 6,
        out_specs=(vmem,) * 3,
        scratch_shapes=[
            pltpu.SemaphoreType.DMA((slots + 4,)),
            pltpu.SMEM(sources.shape, sources.dtype),
            pltpu.SemaphoreType.DMA,
        ],
        compiler_params=limit,
        name="pack",
    )(counts, *in_hbm)

    def swap(value, axis, size, d):
        return lax.ppermute(value, axis, [(i, i ^ d) for i in range(size)])

    def spread(value):
        arrived = [swap(value, "rep", reps, d) for d in range(1, reps)]
        return [value, *arrived]

    def local(kernel, outs, *operands, scratch=()):
        return pl.pallas_call(
            kernel,
            out_shape=outs,
            in_specs=[vmem] * len(operands),
            out_specs=(vmem,) * len(outs),
            scratch_shapes=scratch,
            compiler_params=limit,
        )(*operands)

    def pair(value):
        return value, swap(value, "row", rows, 1)

    third = swap(for_chips, "row", rows, CORES * 3)
    second = swap(for_chips, "row", rows, CORES * 2)
    from_next = swap(for_next, "row", rows, CORES)
    own, third, second = spread(for_reps), spread(third), spread(second)

    outs = (rows_shape, shape((wide, wide), BF16), shape((reps - 1, height, share), BF16))
    own_rows, weight, peers = local(own_kernel, outs, *own, for_next)
    peers = swap(peers, "row", rows, CORES)
    (next_rows,) = local(next_kernel, (rows_shape,), from_next, peers)
    outs = (shape((step, wide), BF16), shape((step, wide + nodes), BF16))
    far_feats, far_rest = local(far_kernel, outs, *second, *third)
    outs = (
        *(bundle_shape, bundle_shape),
        shape((2, wide, wide), BF16),
        shape((2 * CORES, step, wide), F32),
        shape((CORES, step, wide), F32),
    )
    *near_bundles, weights, back, agg = local(
        early_kernel,
        outs,
        *pair(own_rows),
        *pair(next_rows),
        *pair(weight),
        scratch=[pltpu.VMEM((CORES, step, wide), BF16)],
    )
    other_feats = swap(far_feats, "row", rows, 1)
    other_rest = swap(far_rest, "row", rows, 1)
    back, agg = local(
        middle_kernel,
        (shape((2 * CORES, step, wide), F32), shape((CORES + 1, step, wide), F32)),
        *near_bundles,
        *(far_feats, far_rest, weights, back, agg),
    )
    count = CORES + 1
    outs = tuple(shape((count, step, wide), dtype) for dtype in (BF16, BF16, F32))
    first_layer = local(hidden_kernel, outs, *near_bundles, far_rest, other_feats, weights, agg)
    outs = (shape((height, width), BF16), shape((width, wide), F32), shape((width, wide), F32))
    return local(
        functools.partial(layers_kernel, reps, 1.0 / math.sqrt(nodes)),
        outs,
        *near_bundles,
        *(far_feats, far_rest, other_feats, other_rest, weights, back),
        *first_layer,
        scratch=[pltpu.VMEM((step, wide), dtype) for dtype in (BF16, BF16, F32)],
    )


def fits_whole(features, edge_tiles, rows, reps):
    nodes, wide = features.shape
    block = edge_tiles.shape[2]
    powers = all(n & (n - 1) == 0 for n in (rows, reps))
    held = 2 * (nodes * nodes + 2 * nodes * wide + 2 * wide * wide)
    width, share = wide // reps, nodes // reps
    return (
        held <= REPLICATED_BYTES
        and powers
        and rows % CORES == 0
        and nodes // rows == block == width
        and share % block == 0
        and share == 2 * width
        and wide == 2 * share
        and rows == 4 * CORES
    )


def solution(mesh):
    placed = (
        P("row", "rep"),
        P("row", None, None, None),
        P("row", None),
        P("row"),
        P("rep", None),
        P("rep", None),
        P("row", "rep"),
    )

    rows, reps = mesh.shape["row"], mesh.shape["rep"]
    outs = (P("row", "rep"), P("rep", None), P("rep", None))

    def run(features, edge_tiles, *rest):
        whole = fits_whole(features, edge_tiles, rows, reps)

        def body(*args):
            return (whole_body if whole else split_body)(*args)

        step = jax.shard_map(body, mesh=mesh, in_specs=placed, out_specs=outs, check_vma=False)
        return step(features, edge_tiles, *rest)

    return run
```

```python
import functools
import math

import jax
import jax.numpy as jnp
from jax import lax
from jax.experimental import pallas as pl
from jax.experimental.pallas import tpu as pltpu
from jax.sharding import PartitionSpec as P

BF16 = jnp.bfloat16
F32 = jnp.float32
CORES = 2
REPLICATED_BYTES = 16 * 2**20


def silu_slope(value):
    sig = jax.nn.sigmoid(value)
    return sig * (1.0 + value * (1.0 - sig))


def gather_blocks(local, block):
    height, width = local.shape
    packed = local.reshape(height * width // 128, 128)
    whole = lax.all_gather(packed, "row", axis=0, tiled=True)
    return whole.reshape(-1, block, width)


def aggregate(local, live_tiles, sources):
    height, width = local.shape
    _, _, block, _ = live_tiles.shape
    blocks = gather_blocks(local, block)
    total = jnp.einsum(
        "bkij,bkjf->bif", live_tiles, blocks[sources], preferred_element_type=jnp.float32
    )
    return total.reshape(height, width).astype(jnp.bfloat16)


def spread_back(back_agg, live_tiles):
    group_rows, _, block, _ = live_tiles.shape
    width = back_agg.shape[1]
    block_rows = back_agg.reshape(group_rows, block, width)
    return jnp.einsum("bkij,bif->bkjf", live_tiles, block_rows, preferred_element_type=jnp.float32)


def mix_columns(agg, weight):
    partial_terms = jnp.dot(agg, weight, preferred_element_type=jnp.float32)
    return lax.psum_scatter(partial_terms, "rep", scatter_dimension=1, tiled=True)


def widen(local):
    return lax.all_gather(local, "rep", axis=1, tiled=True)


def split_body(features, edge_tiles, sources, counts, w_first, w_second, cotangent):
    group_rows, slots, block, _ = edge_tiles.shape
    height, width = features.shape
    live = jnp.arange(slots, dtype=jnp.int32)[None, :] < counts[:, None]
    live_tiles = edge_tiles * live[:, :, None, None].astype(edge_tiles.dtype)
    scale = 1.0 / math.sqrt(height * lax.axis_size("row"))
    agg_first = aggregate(features, live_tiles, sources)
    pre_first = mix_columns(agg_first, w_first)
    hidden = jax.nn.silu(pre_first).astype(jnp.bfloat16)
    agg_second = aggregate(hidden, live_tiles, sources)
    embeddings = mix_columns(agg_second, w_second).astype(jnp.bfloat16)
    full_cotangent = widen(cotangent)
    second_part = jnp.dot(agg_second.T, full_cotangent, preferred_element_type=jnp.float32) * scale
    back_agg = jnp.dot(full_cotangent, w_second.T, preferred_element_type=jnp.float32).astype(
        jnp.bfloat16
    )
    contrib = spread_back(back_agg, live_tiles)
    flat_sources = sources.reshape(-1)
    flat_contrib = contrib.reshape(group_rows * slots, block * width)
    count = height * lax.axis_size("row")
    wanted = count // block
    inside = (flat_sources >= 0) & (flat_sources < wanted)
    target = jnp.where(inside, flat_sources, wanted)
    summed = jax.ops.segment_sum(flat_contrib, target, num_segments=wanted + 1)
    back_hidden = lax.psum_scatter(
        summed[:wanted].reshape(count, width), "row", scatter_dimension=0, tiled=True
    )
    back_pre = (back_hidden * silu_slope(pre_first)).astype(jnp.bfloat16)
    first_part = jnp.dot(agg_first.T, widen(back_pre), preferred_element_type=jnp.float32) * scale
    grad_second, grad_first = lax.psum((second_part, first_part), "row")
    return (embeddings, grad_first, grad_second)


def dot(a, b, contract):
    return lax.dot_general(a, b, (contract, ((), ())), preferred_element_type=F32)


def pack_kernel(
    chips, parts, counts_ref, sources_hbm, feat_ref, cot_ref, tiles_ref, w1_ref, w2_ref, *outs
):
    for_chips, for_reps, for_next, sems, sources_ref, index_sem = outs
    index_copy = pltpu.make_async_copy(sources_hbm, sources_ref, index_sem)
    index_copy.start()
    _, slots, block, _ = tiles_ref.shape
    width = feat_ref.shape[1]
    core = lax.rem(lax.axis_index("row"), CORES)
    moves = [
        (feat_ref, for_reps.at[0, :, pl.ds(0, width)]),
        (cot_ref, for_reps.at[0, :, pl.ds(width, width)]),
    ]
    copies = [pltpu.make_async_copy(*move, sems.at[slots + n]) for n, move in enumerate(moves)]
    for copy in copies:
        copy.start()
    step = for_reps.shape[2]

    def weight_copy(ref, n):
        lanes = pl.ds(n * step, step)
        return pltpu.make_async_copy(ref.at[:, lanes], for_reps.at[1 + n], sems.at[slots + 2 + n])

    for c, ref in enumerate((w1_ref, w2_ref)):
        for n in range(2):
            pl.when(core == c)(lambda ref=ref, n=n: weight_copy(ref, n).start())
    for_next[1:] = jnp.zeros_like(for_next[1:])
    index_copy.wait()

    def tile_copy(k):
        source = sources_ref[0, k]
        position = lax.rem(source, CORES) * chips + lax.div(source, CORES)
        columns = pl.ds(pl.multiple_of(lax.rem(position, parts) * block, block), block)
        target = for_next.at[1 + lax.div(position, parts), :, columns]
        return pltpu.make_async_copy(tiles_ref.at[0, k], target, sems.at[k])

    for k in range(slots):
        pl.when(k < counts_ref[0])(lambda k=k: tile_copy(k).start())
    for copy in copies:
        copy.wait()
    for_chips[0] = for_reps[0]
    for_next[0] = for_reps[0]
    for k in range(slots):
        pl.when(k < counts_ref[0])(lambda k=k: tile_copy(k).wait())
    for_chips[1] = for_next[1 + lax.axis_index("rep")]
    for c, ref in enumerate((w1_ref, w2_ref)):
        for n in range(2):
            pl.when(core == c)(lambda ref=ref, n=n: weight_copy(ref, n).wait())


def at(index, size, start=0):
    return pl.ds(pl.multiple_of(start + index * size, size), size)


def place_features(out_ref, rows, rep, blocks):
    reps = len(blocks)
    width = blocks[0].shape[1] // 2
    for d, block in enumerate(blocks):
        out_ref[rows, at(rep ^ d, width)] = block[:, :width]
        out_ref[rows, at(rep ^ d, width, width * reps)] = block[:, width:]


def place_adjacency(out_ref, rows, for_next):
    share = for_next.shape[2]
    count = for_next.shape[0] - 1
    start = out_ref.shape[1] - count * share
    for j in range(count):
        out_ref[rows, start + j * share : start + (j + 1) * share] = for_next[1 + j]


def own_kernel(*refs):
    *own, for_next, rows_ref, weight_ref, peers_ref = refs
    rep = lax.axis_index("rep")
    _, height, share = for_next.shape
    everything = pl.ds(0, height)
    place_features(rows_ref, everything, rep, [ref[0] for ref in own])
    place_adjacency(rows_ref, everything, for_next)
    width = weight_ref.shape[0] // len(own)
    for d, ref in enumerate(own):
        for n in range(2):
            weight_ref[at(rep ^ d, width), n * share : (n + 1) * share] = ref[1 + n]
        if d:
            peers_ref[d - 1] = ref[0]


def far_kernel(*refs):
    *blocks, feats_ref, rest_ref = refs
    reps = len(blocks) // 2
    rep = lax.axis_index("rep")
    half = lax.rem(lax.div(lax.axis_index("row"), CORES), 2)
    _, height, share = blocks[0].shape
    width = share // 2
    for parity, chunk in ((half, blocks[:reps]), (1 - half, blocks[reps:])):
        rows = at(parity, height)
        for d, ref in enumerate(chunk):
            feats_ref[rows, at(rep ^ d, width)] = ref[0, :, :width]
            rest_ref[rows, at(rep ^ d, width)] = ref[0, :, width:]
            rest_ref[rows, at(rep ^ d, share, width * reps)] = ref[1]


def place_of(b):
    row = lax.axis_index("row")
    core, chip = lax.rem(row, CORES), lax.div(row, CORES)
    dh, dc = divmod(b, CORES)
    return (core ^ dc) * 2 + (lax.div(chip, 2) ^ dh)


def parts_of(bundle, wide, step):
    feats, rest, start = (*bundle, 0) if isinstance(bundle, tuple) else (bundle, bundle, wide)
    return (
        feats[:, :wide],
        rest[:, start : start + wide],
        lambda b: rest[:, at(place_of(b), step, start + wide)],
    )


def total_of(terms):
    total = None
    for term in terms:
        total = term if total is None else total + term
    return total


def back_aggregates(cotangent, weight):
    return dot(cotangent, weight, ((1,), (1,))).astype(BF16)


def early_kernel(*refs):
    own_rows, from_next, peers, weights = (refs[n : n + 2] for n in range(0, 8, 2))
    refs = refs[8:]
    first_bundle, second_bundle, w_ref, back_ref, agg_ref, ba_s = refs
    bundles = first_bundle, second_bundle
    row, rep = lax.axis_index("row"), lax.axis_index("rep")
    core, half = lax.rem(row, CORES), lax.rem(lax.div(row, CORES), 2)
    height = own_rows[0].shape[0]
    mine, other = at(half, height), at(1 - half, height)
    wide = w_ref.shape[1]
    for c in range(CORES):
        bundles[c][mine, :] = own_rows[c][...]
        blocks = [from_next[c][0]] + [peers[c][d] for d in range(peers[c].shape[0])]
        place_features(bundles[c], other, rep, blocks)
        place_adjacency(bundles[c], other, from_next[c])
        w_ref[core ^ c] = weights[c][...]
    parts = [parts_of(bundle, wide, 2 * height) for bundle in bundles]
    for k, (_, cotangent, _) in enumerate(parts):
        ba_s[k] = back_aggregates(cotangent, w_ref[1])
    for b in range(2 * CORES):
        terms = (dot(a(b), ba_s[k], ((0,), (0,))) for k, (_, _, a) in enumerate(parts))
        back_ref[b] = total_of(terms)
    for b, (_, _, a) in enumerate(parts):
        terms = (dot(a(k), feats, ((1,), (0,))) for k, (feats, _, _) in enumerate(parts))
        agg_ref[b] = total_of(terms)


def middle_kernel(*refs):
    first, second, *far, w_ref, back_in, agg_in, back_ref, agg_ref = refs
    bundles = first, second, tuple(far)
    step = first.shape[0]
    parts = [parts_of(bundle, w_ref.shape[1], step) for bundle in bundles]
    feats, cotangent, a = parts[CORES]
    back_agg = back_aggregates(cotangent, w_ref[1])
    for b in range(2 * CORES):
        back_ref[b] = back_in[b] + dot(a(b), back_agg, ((0,), (0,)))
    for b in range(CORES):
        agg_ref[b] = agg_in[b] + dot(parts[b][2](CORES), feats, ((1,), (0,)))
    agg_ref[CORES] = total_of(dot(a(k), parts[k][0], ((1,), (0,))) for k in range(CORES + 1))


def activate(total, weight, agg_ref, hidden_ref, slope_ref):
    agg = total.astype(BF16)
    agg_ref[...] = agg
    pre = dot(agg, weight, ((1,), (0,)))
    sig = jax.nn.sigmoid(pre)
    hidden_ref[...] = (pre * sig).astype(BF16)
    slope_ref[...] = sig * (1.0 + pre * (1.0 - sig))


def hidden_kernel(*refs):
    first, second, far_rest, feats, w_ref, agg_in, *outs = refs
    step, wide = feats.shape
    bundles = first, second, (None, far_rest)
    for b, bundle in enumerate(bundles):
        rest, start = (bundle[1], wide) if b == CORES else (bundle, 2 * wide)
        columns = rest[:, at(place_of(CORES + 1), step, start)]
        total = agg_in[b] + dot(columns, feats[...], ((1,), (0,)))
        activate(total, w_ref[0], *(out.at[b] for out in outs))


def layers_kernel(reps, scale, *refs):
    first, second, *far, w_ref, back_ref, early_agg, early_hidden, early_slope = refs[:11]
    emb_ref, gf_ref, gs_ref, last_agg, last_hidden, last_slope = refs[11:]
    bundles = first, second, tuple(far[:2]), tuple(far[2:])
    row, rep = lax.axis_index("row"), lax.axis_index("rep")
    chip = lax.div(row, CORES)
    height, width = emb_ref.shape
    wide = width * reps
    step = 2 * height
    count = len(bundles)
    last = count - 1
    my_cols = at(rep, width)
    parts = [parts_of(bundle, wide, step) for bundle in bundles]

    back_agg = back_aggregates(parts[last][1], w_ref[1])
    a = parts[last][2]
    total = total_of(dot(a(k), parts[k][0], ((1,), (0,))) for k in range(count))
    activate(total, w_ref[0], last_agg, last_hidden, last_slope)
    agg_first, hidden, slope = (
        [early.at[b] for b in range(last)] + [late]
        for early, late in (
            (early_agg, last_agg),
            (early_hidden, last_hidden),
            (early_slope, last_slope),
        )
    )

    back_pre, agg_second = [], []
    for b in range(count):
        a = parts[b][2]
        back_hidden = back_ref[b] + dot(parts[last][2](b), back_agg, ((0,), (0,)))
        back_pre.append((back_hidden * slope[b][...]).astype(BF16))
    gf = total_of(
        dot(agg_first[b][:, my_cols], back_pre[b], ((0,), (0,))) for b in range(count)
    )
    gf_ref[...] = gf * scale
    for b in range(count):
        a = parts[b][2]
        agg = total_of(dot(a(k), hidden[k][:, my_cols], ((1,), (0,))) for k in range(count))
        agg_second.append(agg.astype(BF16))
    gs = total_of(dot(agg_second[b], parts[b][1], ((0,), (0,))) for b in range(count))
    gs_ref[...] = gs * scale

    mine = at(lax.rem(chip, 2), height)
    agg = total_of(
        dot(first[mine, at(place_of(k), step, 2 * wide)], hidden[k][...], ((1,), (0,)))
        for k in range(count)
    )
    emb_ref[...] = dot(agg.astype(BF16), w_ref[1, :, my_cols], ((1,), (0,))).astype(BF16)


def whole_body(features, edge_tiles, sources, counts, w_first, w_second, cotangent):
    _, slots, block, _ = edge_tiles.shape
    height, width = features.shape
    rows, reps = lax.axis_size("row"), lax.axis_size("rep")
    chips = rows // CORES
    nodes = height * rows
    share = nodes // reps
    wide = width * reps
    vmem = pl.BlockSpec(memory_space=pltpu.VMEM)
    hbm = pl.BlockSpec(memory_space=pltpu.HBM)
    shape = jax.ShapeDtypeStruct
    step = 2 * height
    rows_shape = shape((height, 2 * wide + nodes), BF16)
    bundle_shape = shape((step, 2 * wide + nodes), BF16)
    limit = pltpu.CompilerParams(vmem_limit_bytes=24 * 2**20)

    in_hbm = [
        pltpu.with_memory_space_constraint(v, pltpu.HBM)
        for v in (sources, features, cotangent, edge_tiles, w_first, w_second)
    ]
    for_chips, for_reps, for_next = pl.pallas_call(
        functools.partial(pack_kernel, chips, share // block),
        out_shape=(
            shape((2, height, share), BF16),
            shape((3, height, share), BF16),
            shape((1 + reps, height, share), BF16),
        ),
        in_specs=[pl.BlockSpec(memory_space=pltpu.SMEM)] + [hbm] * 6,
        out_specs=(vmem,) * 3,
        scratch_shapes=[
            pltpu.SemaphoreType.DMA((slots + 4,)),
            pltpu.SMEM(sources.shape, sources.dtype),
            pltpu.SemaphoreType.DMA,
        ],
        compiler_params=limit,
        name="pack",
    )(counts, *in_hbm)

    def swap(value, axis, size, d):
        return lax.ppermute(value, axis, [(i, i ^ d) for i in range(size)])

    def spread(value):
        arrived = [swap(value, "rep", reps, d) for d in range(1, reps)]
        return [value, *arrived]

    def local(kernel, outs, *operands, scratch=()):
        return pl.pallas_call(
            kernel,
            out_shape=outs,
            in_specs=[vmem] * len(operands),
            out_specs=(vmem,) * len(outs),
            scratch_shapes=scratch,
            compiler_params=limit,
        )(*operands)

    def pair(value):
        return value, swap(value, "row", rows, 1)

    third = swap(for_chips, "row", rows, CORES * 3)
    second = swap(for_chips, "row", rows, CORES * 2)
    from_next = swap(for_next, "row", rows, CORES)
    own, third, second = spread(for_reps), spread(third), spread(second)

    outs = (rows_shape, shape((wide, wide), BF16), shape((reps - 1, height, share), BF16))
    own_rows, weight, peers = local(own_kernel, outs, *own, for_next)
    peers = swap(peers, "row", rows, CORES)
    outs = (shape((step, wide), BF16), shape((step, wide + nodes), BF16))
    far_feats, far_rest = local(far_kernel, outs, *second, *third)
    outs = (
        *(bundle_shape, bundle_shape),
        shape((2, wide, wide), BF16),
        shape((2 * CORES, step, wide), F32),
        shape((CORES, step, wide), F32),
    )
    *near_bundles, weights, back, agg = local(
        early_kernel,
        outs,
        *pair(own_rows),
        *pair(from_next),
        *pair(peers),
        *pair(weight),
        scratch=[pltpu.VMEM((CORES, step, wide), BF16)],
    )
    other_feats = swap(far_feats, "row", rows, 1)
    other_rest = swap(far_rest, "row", rows, 1)
    back, agg = local(
        middle_kernel,
        (shape((2 * CORES, step, wide), F32), shape((CORES + 1, step, wide), F32)),
        *near_bundles,
        *(far_feats, far_rest, weights, back, agg),
    )
    count = CORES + 1
    outs = tuple(shape((count, step, wide), dtype) for dtype in (BF16, BF16, F32))
    first_layer = local(hidden_kernel, outs, *near_bundles, far_rest, other_feats, weights, agg)
    outs = (shape((height, width), BF16), shape((width, wide), F32), shape((width, wide), F32))
    return local(
        functools.partial(layers_kernel, reps, 1.0 / math.sqrt(nodes)),
        outs,
        *near_bundles,
        *(far_feats, far_rest, other_feats, other_rest, weights, back),
        *first_layer,
        scratch=[pltpu.VMEM((step, wide), dtype) for dtype in (BF16, BF16, F32)],
    )


def fits_whole(features, edge_tiles, rows, reps):
    nodes, wide = features.shape
    block = edge_tiles.shape[2]
    powers = all(n & (n - 1) == 0 for n in (rows, reps))
    held = 2 * (nodes * nodes + 2 * nodes * wide + 2 * wide * wide)
    width, share = wide // reps, nodes // reps
    return (
        held <= REPLICATED_BYTES
        and powers
        and rows % CORES == 0
        and nodes // rows == block == width
        and share % block == 0
        and share == 2 * width
        and wide == 2 * share
        and rows == 4 * CORES
    )


def solution(mesh):
    placed = (
        P("row", "rep"),
        P("row", None, None, None),
        P("row", None),
        P("row"),
        P("rep", None),
        P("rep", None),
        P("row", "rep"),
    )

    rows, reps = mesh.shape["row"], mesh.shape["rep"]
    outs = (P("row", "rep"), P("rep", None), P("rep", None))

    def run(features, edge_tiles, *rest):
        whole = fits_whole(features, edge_tiles, rows, reps)

        def body(*args):
            return (whole_body if whole else split_body)(*args)

        step = jax.shard_map(body, mesh=mesh, in_specs=placed, out_specs=outs, check_vma=False)
        return step(features, edge_tiles, *rest)

    return run
```

```python
import functools
import math

import jax
import jax.numpy as jnp
from jax import lax
from jax.experimental import pallas as pl
from jax.experimental.pallas import tpu as pltpu
from jax.sharding import PartitionSpec as P

BF16 = jnp.bfloat16
F32 = jnp.float32
CORES = 2
REPLICATED_BYTES = 16 * 2**20


def silu_slope(value):
    sig = jax.nn.sigmoid(value)
    return sig * (1.0 + value * (1.0 - sig))


def gather_blocks(local, block):
    height, width = local.shape
    packed = local.reshape(height * width // 128, 128)
    whole = lax.all_gather(packed, "row", axis=0, tiled=True)
    return whole.reshape(-1, block, width)


def aggregate(local, live_tiles, sources):
    height, width = local.shape
    _, _, block, _ = live_tiles.shape
    blocks = gather_blocks(local, block)
    total = jnp.einsum(
        "bkij,bkjf->bif", live_tiles, blocks[sources], preferred_element_type=jnp.float32
    )
    return total.reshape(height, width).astype(jnp.bfloat16)


def spread_back(back_agg, live_tiles):
    group_rows, _, block, _ = live_tiles.shape
    width = back_agg.shape[1]
    block_rows = back_agg.reshape(group_rows, block, width)
    return jnp.einsum("bkij,bif->bkjf", live_tiles, block_rows, preferred_element_type=jnp.float32)


def mix_columns(agg, weight):
    partial_terms = jnp.dot(agg, weight, preferred_element_type=jnp.float32)
    return lax.psum_scatter(partial_terms, "rep", scatter_dimension=1, tiled=True)


def widen(local):
    return lax.all_gather(local, "rep", axis=1, tiled=True)


def split_body(features, edge_tiles, sources, counts, w_first, w_second, cotangent):
    group_rows, slots, block, _ = edge_tiles.shape
    height, width = features.shape
    live = jnp.arange(slots, dtype=jnp.int32)[None, :] < counts[:, None]
    live_tiles = edge_tiles * live[:, :, None, None].astype(edge_tiles.dtype)
    scale = 1.0 / math.sqrt(height * lax.axis_size("row"))
    agg_first = aggregate(features, live_tiles, sources)
    pre_first = mix_columns(agg_first, w_first)
    hidden = jax.nn.silu(pre_first).astype(jnp.bfloat16)
    agg_second = aggregate(hidden, live_tiles, sources)
    embeddings = mix_columns(agg_second, w_second).astype(jnp.bfloat16)
    full_cotangent = widen(cotangent)
    second_part = jnp.dot(agg_second.T, full_cotangent, preferred_element_type=jnp.float32) * scale
    back_agg = jnp.dot(full_cotangent, w_second.T, preferred_element_type=jnp.float32).astype(
        jnp.bfloat16
    )
    contrib = spread_back(back_agg, live_tiles)
    flat_sources = sources.reshape(-1)
    flat_contrib = contrib.reshape(group_rows * slots, block * width)
    count = height * lax.axis_size("row")
    wanted = count // block
    inside = (flat_sources >= 0) & (flat_sources < wanted)
    target = jnp.where(inside, flat_sources, wanted)
    summed = jax.ops.segment_sum(flat_contrib, target, num_segments=wanted + 1)
    back_hidden = lax.psum_scatter(
        summed[:wanted].reshape(count, width), "row", scatter_dimension=0, tiled=True
    )
    back_pre = (back_hidden * silu_slope(pre_first)).astype(jnp.bfloat16)
    first_part = jnp.dot(agg_first.T, widen(back_pre), preferred_element_type=jnp.float32) * scale
    grad_second, grad_first = lax.psum((second_part, first_part), "row")
    return (embeddings, grad_first, grad_second)


def dot(a, b, contract):
    return lax.dot_general(a, b, (contract, ((), ())), preferred_element_type=F32)


def pack_kernel(
    chips, parts, counts_ref, sources_hbm, feat_ref, cot_ref, tiles_ref, w1_ref, w2_ref, *outs
):
    for_chips, for_reps, for_next, sems, sources_ref, index_sem, tiles_s = outs
    index_copy = pltpu.make_async_copy(sources_hbm, sources_ref, index_sem)
    index_copy.start()
    _, slots, block, _ = tiles_ref.shape

    def tile_copy(k):
        return pltpu.make_async_copy(tiles_ref.at[0, k], tiles_s.at[k], sems.at[k])

    for k in range(slots):
        pl.when(k < counts_ref[0])(lambda k=k: tile_copy(k).start())
    width = feat_ref.shape[1]
    core = lax.rem(lax.axis_index("row"), CORES)
    moves = [
        (feat_ref, for_reps.at[0, :, pl.ds(0, width)]),
        (cot_ref, for_reps.at[0, :, pl.ds(width, width)]),
    ]
    copies = [pltpu.make_async_copy(*move, sems.at[slots + n]) for n, move in enumerate(moves)]
    for copy in copies:
        copy.start()
    step = for_reps.shape[2]

    def weight_copy(ref, n):
        lanes = pl.ds(n * step, step)
        return pltpu.make_async_copy(ref.at[:, lanes], for_reps.at[1 + n], sems.at[slots + 2 + n])

    for c, ref in enumerate((w1_ref, w2_ref)):
        for n in range(2):
            pl.when(core == c)(lambda ref=ref, n=n: weight_copy(ref, n).start())
    for_next[1:] = jnp.zeros_like(for_next[1:])
    for copy in copies:
        copy.wait()
    for_chips[0] = for_reps[0]
    for_next[0] = for_reps[0]
    index_copy.wait()

    def place(k):
        tile_copy(k).wait()
        source = sources_ref[0, k]
        position = lax.rem(source, CORES) * chips + lax.div(source, CORES)
        columns = at(lax.rem(position, parts), block)
        for_next[1 + lax.div(position, parts), :, columns] = tiles_s[k]

    for k in range(slots):
        pl.when(k < counts_ref[0])(lambda k=k: place(k))
    for_chips[1] = for_next[1 + lax.axis_index("rep")]
    for c, ref in enumerate((w1_ref, w2_ref)):
        for n in range(2):
            pl.when(core == c)(lambda ref=ref, n=n: weight_copy(ref, n).wait())


def at(index, size, start=0):
    return pl.ds(pl.multiple_of(start + index * size, size), size)


def place_features(out_ref, rows, rep, blocks):
    reps = len(blocks)
    width = blocks[0].shape[1] // 2
    for d, block in enumerate(blocks):
        out_ref[rows, at(rep ^ d, width)] = block[:, :width]
        out_ref[rows, at(rep ^ d, width, width * reps)] = block[:, width:]


def place_adjacency(out_ref, rows, for_next):
    share = for_next.shape[2]
    count = for_next.shape[0] - 1
    start = out_ref.shape[1] - count * share
    for j in range(count):
        out_ref[rows, start + j * share : start + (j + 1) * share] = for_next[1 + j]


def own_kernel(*refs):
    *own, for_next, rows_ref, weight_ref, peers_ref = refs
    rep = lax.axis_index("rep")
    _, height, share = for_next.shape
    everything = pl.ds(0, height)
    place_features(rows_ref, everything, rep, [ref[0] for ref in own])
    place_adjacency(rows_ref, everything, for_next)
    width = weight_ref.shape[0] // len(own)
    for d, ref in enumerate(own):
        for n in range(2):
            weight_ref[at(rep ^ d, width), n * share : (n + 1) * share] = ref[1 + n]
        if d:
            peers_ref[d - 1] = ref[0]


def far_kernel(*refs):
    *blocks, feats_ref, rest_ref = refs
    reps = len(blocks) // 2
    rep = lax.axis_index("rep")
    half = lax.rem(lax.div(lax.axis_index("row"), CORES), 2)
    _, height, share = blocks[0].shape
    width = share // 2
    for parity, chunk in ((half, blocks[:reps]), (1 - half, blocks[reps:])):
        rows = at(parity, height)
        for d, ref in enumerate(chunk):
            feats_ref[rows, at(rep ^ d, width)] = ref[0, :, :width]
            rest_ref[rows, at(rep ^ d, width)] = ref[0, :, width:]
            rest_ref[rows, at(rep ^ d, share, width * reps)] = ref[1]


def place_of(b):
    row = lax.axis_index("row")
    core, chip = lax.rem(row, CORES), lax.div(row, CORES)
    dh, dc = divmod(b, CORES)
    return (core ^ dc) * 2 + (lax.div(chip, 2) ^ dh)


def parts_of(bundle, wide, step):
    feats, rest, start = (*bundle, 0) if isinstance(bundle, tuple) else (bundle, bundle, wide)
    return (
        feats[:, :wide],
        rest[:, start : start + wide],
        lambda b: rest[:, at(place_of(b), step, start + wide)],
    )


def total_of(terms):
    total = None
    for term in terms:
        total = term if total is None else total + term
    return total


def back_aggregates(cotangent, weight):
    return dot(cotangent, weight, ((1,), (1,))).astype(BF16)


def early_kernel(*refs):
    own_rows, from_next, peers, weights = (refs[n : n + 2] for n in range(0, 8, 2))
    refs = refs[8:]
    first_bundle, second_bundle, w_ref, back_ref, agg_ref, ba_s = refs
    bundles = first_bundle, second_bundle
    row, rep = lax.axis_index("row"), lax.axis_index("rep")
    core, half = lax.rem(row, CORES), lax.rem(lax.div(row, CORES), 2)
    height = own_rows[0].shape[0]
    mine, other = at(half, height), at(1 - half, height)
    wide = w_ref.shape[1]
    for c in range(CORES):
        bundles[c][mine, :] = own_rows[c][...]
        blocks = [from_next[c][0]] + [peers[c][d] for d in range(peers[c].shape[0])]
        place_features(bundles[c], other, rep, blocks)
        place_adjacency(bundles[c], other, from_next[c])
        w_ref[core ^ c] = weights[c][...]
    parts = [parts_of(bundle, wide, 2 * height) for bundle in bundles]
    for k, (_, cotangent, _) in enumerate(parts):
        ba_s[k] = back_aggregates(cotangent, w_ref[1])
    for b, (_, _, a) in enumerate(parts):
        terms = (dot(a(k), feats, ((1,), (0,))) for k, (feats, _, _) in enumerate(parts))
        agg_ref[b] = total_of(terms)
    for b in range(2 * CORES):
        terms = (dot(a(b), ba_s[k], ((0,), (0,))) for k, (_, _, a) in enumerate(parts))
        back_ref[b] = total_of(terms)


def middle_kernel(*refs):
    first, second, *far, w_ref, back_in, agg_in, back_ref, agg_ref = refs
    bundles = first, second, tuple(far)
    step = first.shape[0]
    parts = [parts_of(bundle, w_ref.shape[1], step) for bundle in bundles]
    feats, cotangent, a = parts[CORES]
    back_agg = back_aggregates(cotangent, w_ref[1])
    for b in range(CORES):
        agg_ref[b] = agg_in[b] + dot(parts[b][2](CORES), feats, ((1,), (0,)))
    agg_ref[CORES] = total_of(dot(a(k), parts[k][0], ((1,), (0,))) for k in range(CORES + 1))
    for b in range(2 * CORES):
        back_ref[b] = back_in[b] + dot(a(b), back_agg, ((0,), (0,)))


def activate(total, weight, agg_ref, hidden_ref, slope_ref):
    agg = total.astype(BF16)
    agg_ref[...] = agg
    pre = dot(agg, weight, ((1,), (0,)))
    sig = jax.nn.sigmoid(pre)
    hidden_ref[...] = (pre * sig).astype(BF16)
    slope_ref[...] = sig * (1.0 + pre * (1.0 - sig))


def hidden_kernel(*refs):
    first, second, far_rest, feats, w_ref, agg_in, *outs = refs
    step, wide = feats.shape
    bundles = first, second, (None, far_rest)
    for b, bundle in enumerate(bundles):
        rest, start = (bundle[1], wide) if b == CORES else (bundle, 2 * wide)
        columns = rest[:, at(place_of(CORES + 1), step, start)]
        total = agg_in[b] + dot(columns, feats[...], ((1,), (0,)))
        activate(total, w_ref[0], *(out.at[b] for out in outs))


def layers_kernel(reps, scale, *refs):
    first, second, *far, w_ref, back_ref, early_agg, early_hidden, early_slope = refs[:11]
    emb_ref, gf_ref, gs_ref, last_agg, last_hidden, last_slope = refs[11:]
    bundles = first, second, tuple(far[:2]), tuple(far[2:])
    row, rep = lax.axis_index("row"), lax.axis_index("rep")
    chip = lax.div(row, CORES)
    height, width = emb_ref.shape
    wide = width * reps
    step = 2 * height
    count = len(bundles)
    last = count - 1
    my_cols = at(rep, width)
    parts = [parts_of(bundle, wide, step) for bundle in bundles]

    back_agg = back_aggregates(parts[last][1], w_ref[1])
    a = parts[last][2]
    total = total_of(dot(a(k), parts[k][0], ((1,), (0,))) for k in range(count))
    activate(total, w_ref[0], last_agg, last_hidden, last_slope)
    agg_first, hidden, slope = (
        [early.at[b] for b in range(last)] + [late]
        for early, late in (
            (early_agg, last_agg),
            (early_hidden, last_hidden),
            (early_slope, last_slope),
        )
    )

    back_pre, agg_second = [], []
    for b in range(count):
        a = parts[b][2]
        agg = total_of(dot(a(k), hidden[k][:, my_cols], ((1,), (0,))) for k in range(count))
        agg_second.append(agg.astype(BF16))
        back_hidden = back_ref[b] + dot(parts[last][2](b), back_agg, ((0,), (0,)))
        back_pre.append((back_hidden * slope[b][...]).astype(BF16))
    gf = total_of(
        dot(agg_first[b][:, my_cols], back_pre[b], ((0,), (0,))) for b in range(count)
    )
    gf_ref[...] = gf * scale
    gs = total_of(dot(agg_second[b], parts[b][1], ((0,), (0,))) for b in range(count))
    gs_ref[...] = gs * scale

    mine = at(lax.rem(chip, 2), height)
    agg = total_of(
        dot(first[mine, at(place_of(k), step, 2 * wide)], hidden[k][...], ((1,), (0,)))
        for k in range(count)
    )
    emb_ref[...] = dot(agg.astype(BF16), w_ref[1, :, my_cols], ((1,), (0,))).astype(BF16)


def whole_body(features, edge_tiles, sources, counts, w_first, w_second, cotangent):
    _, slots, block, _ = edge_tiles.shape
    height, width = features.shape
    rows, reps = lax.axis_size("row"), lax.axis_size("rep")
    chips = rows // CORES
    nodes = height * rows
    share = nodes // reps
    wide = width * reps
    vmem = pl.BlockSpec(memory_space=pltpu.VMEM)
    hbm = pl.BlockSpec(memory_space=pltpu.HBM)
    shape = jax.ShapeDtypeStruct
    step = 2 * height
    rows_shape = shape((height, 2 * wide + nodes), BF16)
    bundle_shape = shape((step, 2 * wide + nodes), BF16)
    limit = pltpu.CompilerParams(vmem_limit_bytes=24 * 2**20)

    in_hbm = [
        pltpu.with_memory_space_constraint(v, pltpu.HBM)
        for v in (sources, features, cotangent, edge_tiles, w_first, w_second)
    ]
    for_chips, for_reps, for_next = pl.pallas_call(
        functools.partial(pack_kernel, chips, share // block),
        out_shape=(
            shape((2, height, share), BF16),
            shape((3, height, share), BF16),
            shape((1 + reps, height, share), BF16),
        ),
        in_specs=[pl.BlockSpec(memory_space=pltpu.SMEM)] + [hbm] * 6,
        out_specs=(vmem,) * 3,
        scratch_shapes=[
            pltpu.SemaphoreType.DMA((slots + 4,)),
            pltpu.SMEM(sources.shape, sources.dtype),
            pltpu.SemaphoreType.DMA,
            pltpu.VMEM(edge_tiles.shape[1:], BF16),
        ],
        compiler_params=limit,
        name="pack",
    )(counts, *in_hbm)

    def swap(value, axis, size, d):
        return lax.ppermute(value, axis, [(i, i ^ d) for i in range(size)])

    def spread(value):
        arrived = [swap(value, "rep", reps, d) for d in range(1, reps)]
        return [value, *arrived]

    def local(kernel, outs, *operands, scratch=()):
        return pl.pallas_call(
            kernel,
            out_shape=outs,
            in_specs=[vmem] * len(operands),
            out_specs=(vmem,) * len(outs),
            scratch_shapes=scratch,
            compiler_params=limit,
        )(*operands)

    def pair(value):
        return value, swap(value, "row", rows, 1)

    third = swap(for_chips, "row", rows, CORES * 3)
    second = swap(for_chips, "row", rows, CORES * 2)
    from_next = swap(for_next, "row", rows, CORES)
    own, third, second = spread(for_reps), spread(third), spread(second)

    outs = (rows_shape, shape((wide, wide), BF16), shape((reps - 1, height, share), BF16))
    own_rows, weight, peers = local(own_kernel, outs, *own, for_next)
    peers = swap(peers, "row", rows, CORES)
    outs = (shape((step, wide), BF16), shape((step, wide + nodes), BF16))
    far_feats, far_rest = local(far_kernel, outs, *second, *third)
    outs = (
        *(bundle_shape, bundle_shape),
        shape((2, wide, wide), BF16),
        shape((2 * CORES, step, wide), F32),
        shape((CORES, step, wide), F32),
    )
    *near_bundles, weights, back, agg = local(
        early_kernel,
        outs,
        *pair(own_rows),
        *pair(from_next),
        *pair(peers),
        *pair(weight),
        scratch=[pltpu.VMEM((CORES, step, wide), BF16)],
    )
    other_feats = swap(far_feats, "row", rows, 1)
    other_rest = swap(far_rest, "row", rows, 1)
    back, agg = local(
        middle_kernel,
        (shape((2 * CORES, step, wide), F32), shape((CORES + 1, step, wide), F32)),
        *near_bundles,
        *(far_feats, far_rest, weights, back, agg),
    )
    count = CORES + 1
    outs = tuple(shape((count, step, wide), dtype) for dtype in (BF16, BF16, F32))
    first_layer = local(hidden_kernel, outs, *near_bundles, far_rest, other_feats, weights, agg)
    outs = (shape((height, width), BF16), shape((width, wide), F32), shape((width, wide), F32))
    return local(
        functools.partial(layers_kernel, reps, 1.0 / math.sqrt(nodes)),
        outs,
        *near_bundles,
        *(far_feats, far_rest, other_feats, other_rest, weights, back),
        *first_layer,
        scratch=[pltpu.VMEM((step, wide), dtype) for dtype in (BF16, BF16, F32)],
    )


def fits_whole(features, edge_tiles, rows, reps):
    nodes, wide = features.shape
    block = edge_tiles.shape[2]
    powers = all(n & (n - 1) == 0 for n in (rows, reps))
    held = 2 * (nodes * nodes + 2 * nodes * wide + 2 * wide * wide)
    width, share = wide // reps, nodes // reps
    return (
        held <= REPLICATED_BYTES
        and powers
        and rows % CORES == 0
        and nodes // rows == block == width
        and share % block == 0
        and share == 2 * width
        and wide == 2 * share
        and rows == 4 * CORES
    )


def solution(mesh):
    placed = (
        P("row", "rep"),
        P("row", None, None, None),
        P("row", None),
        P("row"),
        P("rep", None),
        P("rep", None),
        P("row", "rep"),
    )

    rows, reps = mesh.shape["row"], mesh.shape["rep"]
    outs = (P("row", "rep"), P("rep", None), P("rep", None))

    def run(features, edge_tiles, *rest):
        whole = fits_whole(features, edge_tiles, rows, reps)

        def body(*args):
            return (whole_body if whole else split_body)(*args)

        step = jax.shard_map(body, mesh=mesh, in_specs=placed, out_specs=outs, check_vma=False)
        return step(features, edge_tiles, *rest)

    return run
```
